32 devices in a mesh: vocab: 4 (over z), rows: 8 (over y, x, core).
Axes of the slice: x: 2, y: 2, z: 4, core: 2. Of those that a mesh axis runs over, the one named last changes fastest.
Arguments:
- hidden_pass: bfloat16 [96, 64, 4096], P('rows', None, 'vocab'), may hold values from -6 to 6
- hidden_query: bfloat16 [96, 8, 4096], P('rows', None, 'vocab'), may hold values from -6 to 6
- mask_pass: int32 [96, 64], P('rows'), may hold values 0 or 1
- mask_query: int32 [96, 8], P('rows'), may hold values 0 or 1
- labels: int32 [96], P('rows'), may hold values from 0 to 95, each once
- head_weight: bfloat16 [4096, 16384], P('rows', 'vocab'), may hold values from -1 to 1
Outputs:
- grad_pass: bfloat16 [96, 64, 4096], P('rows', None, 'vocab')
- grad_query: bfloat16 [96, 8, 4096], P('rows', None, 'vocab')
The draws below stay inside these ranges and needn't reach their ends.
Inputs may be any that keep to these rules, and one draw needn't show every extreme that they name: `labels`: each passage is the positive of exactly one query.
All inputs are finite; a program needn't handle non-finite values. No bound on the sum of `mask_pass` or of `mask_query` on one device may be relied on, other than what follows from the above.
Results may differ from the reference program's by a relative error of at most 0.018.
The reference program's roundings to bfloat16 on the way count: a program that leaves them out, or rounds other values in their place, can miss the bound.
Values may be sent and summed in bfloat16 or wider, within the bound.
No kernel may reach another device: no remote copies, remote signals or barrier semaphores. Data moves between devices by JAX's collectives and lax.ppermute only.
A program may use at most 128 MiB of HBM per device.

```python
import jax
import jax.numpy as jnp
from jax import lax

D = 4096
V = 16384
LP = 64
LQ = 8
ROW_DEV = 12
PASSAGES = 96
QUERIES = 96
N_VOCAB = 4


def draw_head_weight(key, part):
    entry_key = jax.random.fold_in(key, 11)
    column_key = jax.random.fold_in(key, 12)
    position = jnp.arange(V, dtype=jnp.float32)[None, :] / V
    rough = jnp.exp(jax.random.uniform(column_key, (1, V), jnp.float32, jnp.log(0.7), jnp.log(1.4)))
    entries = jnp.clip(jax.random.normal(entry_key, (D, V), jnp.float32), -6.0, 6.0)
    ramp = 0.5 * jnp.exp(position * jnp.log(8.0))
    values = jnp.clip(entries * D ** (-0.5) * ramp * rough, -1.0, 1.0)
    return values.astype(jnp.bfloat16)


def plant(values, stream_key, least, top_value):
    index_at = [jax.random.randint(jax.random.fold_in(stream_key, axis), (), 0, length) for axis, length in enumerate(values.shape)]
    main_axis = values.shape.index(max(values.shape))
    neighbour = index_at[:main_axis] + [(index_at[main_axis] + 1) % values.shape[main_axis]] + index_at[main_axis + 1:]
    return values.at[tuple(index_at)].set(least).at[tuple(neighbour)].set(top_value)


def steps_of(own_key, dims, cuts, least, high):
    gain = 1.0
    for dim, blocks in cuts:
        draws = jax.random.uniform(jax.random.fold_in(jax.random.fold_in(own_key, 6), dim), (blocks,), jnp.float32, least / len(cuts), high / len(cuts))
        gain = gain * jnp.repeat(jnp.exp(draws), dims[dim] // blocks).reshape((-1,) + (1,) * (len(dims) - 1 - dim))
    return gain


def bell_draw(own_key, extent, width, bound, pieces=(), kind=jnp.bfloat16):
    result = jax.random.normal(own_key, extent, jnp.float32) * width
    if len(pieces) > 0:
        result = steps_of(own_key, extent, pieces, -0.22, 0.18) * result
    return jnp.clip(result, min=-bound, max=bound).astype(kind)


def setup_inputs(seed: int = 0) -> dict:
    streams_of = jax.random.split(jax.random.key(seed), 7)
    return {
        "hidden_pass": bell_draw(streams_of[0], (PASSAGES, LP, D), 1.0, 6.0, ((0, 8), (2, 4))),
        "hidden_query": bell_draw(streams_of[1], (QUERIES, LQ, D), 1.0, 6.0, ((0, 8), (2, 4))),
        "mask_pass": plant((jax.random.randint(streams_of[2], (PASSAGES, LP), 0, 4) < 3).astype(jnp.int32), jax.random.fold_in(streams_of[2], 1), 0, 1),
        "mask_query": plant((jax.random.randint(streams_of[3], (QUERIES, LQ), 0, 4) < 3).astype(jnp.int32), jax.random.fold_in(streams_of[3], 1), 0, 1),
        "labels": jax.random.permutation(streams_of[4], PASSAGES).astype(jnp.int32),
        "head_weight": draw_head_weight(jax.random.fold_in(streams_of[6], 71), 0),
    }


MARGIN = 1.0
SHARPNESS = 16.0

def activate(logits):
    return jnp.log1p(jnp.maximum(logits, 0.0))

def pool_rows(logits, mask, groups, length):
    values = activate(logits).reshape(groups, length, -1)
    weight = mask.astype(jnp.float32)[:, :, None]
    totals = lax.optimization_barrier(jnp.sum(values ** 4 * weight, axis=1))
    sparse = (jnp.power(totals + 1.0, 0.25) - 1.0).astype(jnp.bfloat16)
    return (values, totals, sparse)

def logit_slopes(sparse_grad, values, totals, logits, mask, groups, length):
    weight = mask.astype(jnp.float32)[:, :, None]
    factor = sparse_grad * jnp.power(totals + 1.0, -0.75)
    slopes = 1.0 / (1.0 + jnp.maximum(logits, 0.0)).reshape(groups, length, -1)
    gradient = factor[:, None, :] * weight * values ** 3 * slopes
    return gradient.astype(jnp.bfloat16).reshape(groups * length, -1)

def side_logits(hidden, head_weight):
    return jnp.dot(hidden.reshape(hidden.shape[0] * hidden.shape[1], hidden.shape[2]), head_weight, preferred_element_type=jnp.float32)

def side_sparse(hidden, mask, head_weight):
    blocks = hidden.shape[0] // ROW_DEV

    def single(bundle):
        block_hidden, block_mask = bundle
        logits = side_logits(block_hidden, head_weight)
        return pool_rows(logits, block_mask, ROW_DEV, block_hidden.shape[1])[2]
    stacked = lax.map(single, (hidden.reshape(blocks, ROW_DEV, hidden.shape[1], hidden.shape[2]), mask.reshape(blocks, ROW_DEV, mask.shape[1])))
    return stacked.reshape(hidden.shape[0], -1)

def side_grad(hidden, mask, sparse_grad, head_weight):
    blocks = hidden.shape[0] // ROW_DEV
    slice_width = V // N_VOCAB

    def single(bundle):
        block_hidden, block_mask, block_grad = bundle
        length = block_hidden.shape[1]
        logits = side_logits(block_hidden, head_weight)
        values, totals, unused_sparse = pool_rows(logits, block_mask, ROW_DEV, length)
        slopes = logit_slopes(block_grad, values, totals, logits, block_mask, ROW_DEV, length)
        summed = jnp.zeros((ROW_DEV * length, D), jnp.float32)
        for slice_index in range(N_VOCAB):
            lower = slice_index * slice_width
            upper = lower + slice_width
            partial_value = lax.dot_general(slopes[:, lower:upper], head_weight[:, lower:upper], (((1,), (1,)), ((), ())), preferred_element_type=jnp.float32)
            summed = summed + lax.optimization_barrier(partial_value.astype(jnp.bfloat16)).astype(jnp.float32)
        return summed.astype(jnp.bfloat16).reshape(ROW_DEV, length, D)
    stacked = lax.map(single, (hidden.reshape(blocks, ROW_DEV, hidden.shape[1], hidden.shape[2]), mask.reshape(blocks, ROW_DEV, mask.shape[1]), sparse_grad.reshape(blocks, ROW_DEV, sparse_grad.shape[1])))
    return stacked.reshape(hidden.shape)

def reference(hidden_pass, hidden_query, mask_pass, mask_query, labels, head_weight):
    sparse_pass = side_sparse(hidden_pass, mask_pass, head_weight)
    sparse_query = side_sparse(hidden_query, mask_query, head_weight)
    scaling = SHARPNESS * V ** (-0.5)
    scores = jnp.dot(sparse_query, sparse_pass.T, preferred_element_type=jnp.float32) * scaling
    onehot = (labels[:, None] == jnp.arange(sparse_pass.shape[0], dtype=jnp.int32)[None, :]).astype(jnp.float32)
    positive = lax.optimization_barrier(jnp.sum(scores * onehot, axis=1, keepdims=True))
    weights = jax.nn.sigmoid(MARGIN + scores - positive) * (1.0 - onehot)
    score_grad = ((weights - onehot * lax.optimization_barrier(jnp.sum(weights, axis=1, keepdims=True))) * scaling).astype(jnp.bfloat16)
    query_sparse_grad = jnp.dot(score_grad, sparse_pass, preferred_element_type=jnp.float32)
    pass_sparse_grad = jnp.dot(score_grad.T, sparse_query, preferred_element_type=jnp.float32)
    grad_pass = side_grad(hidden_pass, mask_pass, pass_sparse_grad, head_weight)
    grad_query = side_grad(hidden_query, mask_query, query_sparse_grad, head_weight)
    return (grad_pass, grad_query)
```

```python
import functools

import jax
import jax.numpy as jnp
from jax import lax
from jax.experimental import pallas as pl
from jax.experimental.pallas import tpu as pltpu
from jax.sharding import PartitionSpec as P

MARGIN = 1.0
SHARPNESS = 16.0

CORES = 2


def chip_grid(n_rows):
    chips = n_rows // CORES
    tall = 1
    while (tall * 2) ** 2 <= chips and chips % (tall * 2) == 0:
        tall *= 2
    return tall, chips // tall


def line_gather(block, n):
    found = {0: block}
    left = right = block
    for step in range(1, n):
        left = lax.ppermute(left, "vocab", [(z, z - 1) for z in range(1, n - step + 1)])
        right = lax.ppermute(right, "vocab", [(z, z + 1) for z in range(step - 1, n - 1)])
        found[step] = left
        found[-step] = right
    return found


def head_pieces(head, n_rows):
    me = lax.axis_index("rows")
    tall, wide = chip_grid(n_rows)
    if (tall, wide) != (2, 2):
        whole = lax.all_gather(head, "rows", axis=0)
        return [whole[r] for r in range(n_rows)], [jnp.int32(r) for r in range(n_rows)]
    x_bit, y_bit = CORES, CORES * wide
    main = [(r, r ^ (x_bit if r % CORES == 0 else y_bit)) for r in range(n_rows)]
    side = [(r, r ^ (y_bit if r % CORES == 0 else x_bit)) for r in range(n_rows)]
    twin = [(r, r ^ 1) for r in range(n_rows)]
    first = me % CORES == 0
    main_of = lambda r, even: r ^ jnp.where(even, x_bit, y_bit)
    side_of = lambda r, even: r ^ jnp.where(even, y_bit, x_bit)
    by_main = lax.ppermute(head, "rows", main)
    by_side = lax.ppermute(head, "rows", side)
    head_twin = lax.ppermute(head, "rows", twin)
    far = lax.ppermute(by_side, "rows", main)
    main_twin = lax.ppermute(by_main, "rows", twin)
    side_twin = lax.ppermute(by_side, "rows", twin)
    far_twin = lax.ppermute(far, "rows", twin)
    pieces = [head, head_twin, by_main, main_twin, by_side, side_twin, far, far_twin]
    other = me ^ 1
    at = [
        me,
        other,
        main_of(me, first),
        main_of(other, ~first),
        side_of(me, first),
        side_of(other, ~first),
        me ^ (x_bit | y_bit),
        other ^ (x_bit | y_bit),
    ]
    return pieces, at


def load_hidden(codes_ref, offs_ref, sources, held, sem, count, depth):
    def copies(t):
        for code, ref in sources:
            yield code, pltpu.make_async_copy(
                ref.at[:, pl.ds(pl.multiple_of(offs_ref[t], 128), depth)], held.at[t], sem.at[t]
            )

    for t in range(count):
        for code, copy in copies(t):
            pl.when(codes_ref[t] == code)(copy.start)
    for t in range(count):
        next(copies(t))[1].wait()


def pooled(x, mask, groups):
    length = x.shape[0] // groups
    u = 1.0 + x
    inverse = 1.0 / u
    act = jnp.log(u) + (x - (u - 1.0)) * inverse
    square = act * act
    total = jnp.sum((square * square * mask).reshape(groups, length, -1), axis=1)
    return total, square * act * inverse * mask


def forward_kernel(spec, codes_ref, offs_ref, *refs):
    count, codes, depth, has_total, final, groups, pass_rows = spec
    refs = list(refs)
    sources = [(code, refs.pop(0)) for code in codes]
    pieces = [refs.pop(0) for _ in range(count)]
    start_ref = refs.pop(0) if has_total else None
    mask_ref = refs.pop(0) if final else None
    if final:
        slope_ref, total_pass_ref, total_query_ref, pass_ref, query_ref = [refs.pop(0) for _ in range(5)]
    else:
        out_ref = refs.pop(0)
    held, sem = refs

    @pl.when(pl.program_id(0) == 0)
    def _():
        load_hidden(codes_ref, offs_ref, sources, held, sem, count, depth)

    value = start_ref[...] if has_total else None
    for t in range(count):
        term = jnp.dot(held[t], pieces[t][...], preferred_element_type=jnp.float32)
        value = term if value is None else value + term
    if not final:
        out_ref[...] = value
        return
    x = jnp.maximum(value, 0.0)
    mask = mask_ref[...]
    width = x.shape[1]
    mask = jnp.concatenate([mask] * (width // mask.shape[1]), axis=1)
    for lower, upper, total_ref, sparse_ref in (
        (0, pass_rows, total_pass_ref, pass_ref),
        (pass_rows, x.shape[0], total_query_ref, query_ref),
    ):
        total, slope = pooled(x[lower:upper], mask[lower:upper], groups)
        slope_ref[lower:upper, :] = slope.astype(slope_ref.dtype)
        total_ref[...] = total
        sparse_ref[...] = (jnp.sqrt(jnp.sqrt(total + 1.0)) - 1.0).astype(sparse_ref.dtype)


def forward(found, pieces, at, n_vocab, start=None, mask=None, groups=0, pass_rows=0, tile=512):
    rows = found[0].shape[0]
    depth, width = pieces[0].shape
    share = found[0].shape[1] // depth
    z = lax.axis_index("vocab")
    at = jnp.stack(at).astype(jnp.int32)
    codes = at // share - z
    offs = at % share * depth
    count = len(pieces)
    keys = sorted(found)
    final = mask is not None
    anywhere = pl.BlockSpec(memory_space=pl.ANY)
    column = lambda height: pl.BlockSpec((height, tile), lambda j, *_: (0, j))
    operands = [found[key] for key in keys] + list(pieces)
    in_specs = [anywhere] * len(keys) + [column(depth)] * count
    if start is not None:
        operands.append(start)
        in_specs.append(column(rows))
    if final:
        operands.append(mask)
        in_specs.append(pl.BlockSpec(mask.shape, lambda j, *_: (0, 0)))
        out_shape = [
            jax.ShapeDtypeStruct((rows, width), jnp.bfloat16),
            jax.ShapeDtypeStruct((groups, width), jnp.float32),
            jax.ShapeDtypeStruct((groups, width), jnp.float32),
            jax.ShapeDtypeStruct((groups, width), jnp.bfloat16),
            jax.ShapeDtypeStruct((groups, width), jnp.bfloat16),
        ]
        out_specs = [column(rows)] + [column(groups)] * 4
    else:
        out_shape = jax.ShapeDtypeStruct((rows, width), jnp.float32)
        out_specs = column(rows)
    spec = (count, tuple(keys), depth, start is not None, final, groups, pass_rows)
    return pl.pallas_call(
        functools.partial(forward_kernel, spec),
        out_shape=out_shape,
        grid_spec=pltpu.PrefetchScalarGridSpec(
            num_scalar_prefetch=2,
            grid=(width // tile,),
            in_specs=in_specs,
            out_specs=out_specs,
            scratch_shapes=[
                pltpu.VMEM((count, rows, depth), jnp.bfloat16),
                pltpu.SemaphoreType.DMA((count,)),
            ],
        ),
        compiler_params=pltpu.CompilerParams(
            dimension_semantics=("arbitrary",), vmem_limit_bytes=50 * 1024 * 1024
        ),
        cost_estimate=pl.CostEstimate(
            flops=2 * rows * depth * count * width,
            bytes_accessed=count * depth * width * 2 + rows * width * 8,
            transcendentals=rows * width if final else 0,
        ),
        name="forward_final" if final else "forward_part",
    )(codes, offs, *operands)


def backward_kernel(count, parts, order_ref, slopes_ref, *refs):
    pieces, (out_ref, held, sem) = refs[:count], refs[count:]
    unit = pl.program_id(0)

    def fetch(which, slot, action):
        for j in range(count):
            copy = pltpu.make_async_copy(pieces[j], held.at[slot], sem.at[slot])
            pl.when(order_ref[which] == j)(copy.start)

    @pl.when(unit == 0)
    def _():
        fetch(0, 0, None)

    slot = lax.rem(unit, 2)

    @pl.when(unit + 1 < pl.num_programs(0))
    def _():
        fetch(unit + 1, 1 - slot, None)

    pltpu.make_async_copy(pieces[0], held.at[slot], sem.at[slot]).wait()
    rows = slopes_ref.shape[0] // parts

    @pl.loop(0, parts)
    def _(i):
        at = pl.ds(pl.multiple_of(i * rows, 16), rows)
        out_ref[0, at, :] = lax.dot_general(
            slopes_ref[at, :], held[slot], (((1,), (1,)), ((), ())), preferred_element_type=jnp.float32
        ).astype(out_ref.dtype)


def backward(slopes, pieces, order):
    rows, width = slopes.shape
    depth = pieces[0].shape[0]
    count = len(pieces)
    units = order.shape[0]
    parts = 3 if rows % 48 == 0 else 1
    return pl.pallas_call(
        functools.partial(backward_kernel, count, parts),
        out_shape=jax.ShapeDtypeStruct((units, rows, depth), jnp.bfloat16),
        grid_spec=pltpu.PrefetchScalarGridSpec(
            num_scalar_prefetch=1,
            grid=(units,),
            in_specs=[
                pl.BlockSpec((rows, width), lambda u, *_: (0, 0), pipeline_mode=pl.Buffered(1))
            ]
            + [pl.BlockSpec(memory_space=pl.ANY)] * count,
            out_specs=pl.BlockSpec((1, rows, depth), lambda u, *_: (u, 0, 0)),
            scratch_shapes=[
                pltpu.VMEM((2, depth, width), jnp.bfloat16),
                pltpu.SemaphoreType.DMA((2,)),
            ],
        ),
        compiler_params=pltpu.CompilerParams(
            dimension_semantics=("arbitrary",), vmem_limit_bytes=50 * 1024 * 1024
        ),
        cost_estimate=pl.CostEstimate(
            flops=2 * rows * depth * units * width,
            bytes_accessed=(units * depth * width + rows * width + units * rows * depth) * 2,
            transcendentals=0,
        ),
        name="backward_part",
    )(order, slopes, *pieces)


def line_reduce_scatter(partial_of, n):
    z = lax.axis_index("vocab")
    left = right = None
    for step in range(1, n):
        if 2 * step <= n:
            block = partial_of(jnp.where(z + step >= n, z + step - n, (z - step) % n))
            to_left, to_right = block, block
        else:
            to_left = partial_of((z + step) % n)
            to_right = partial_of((z - step) % n)
        if left is not None:
            to_left = [(a.astype(jnp.float32) + b.astype(jnp.float32)).astype(a.dtype) for a, b in zip(to_left, left)]
            to_right = [(a.astype(jnp.float32) + b.astype(jnp.float32)).astype(a.dtype) for a, b in zip(to_right, right)]
        left = [lax.ppermute(a, "vocab", [(d, d - 1) for d in range(n - step, n)]) for a in to_left]
        right = [lax.ppermute(a, "vocab", [(d, d + 1) for d in range(step)]) for a in to_right]
    own = partial_of(z)
    return [
        a.astype(jnp.float32) + b.astype(jnp.float32) + c.astype(jnp.float32)
        for a, b, c in zip(own, left, right)
    ]


def shards(n_vocab, n_rows, hidden_pass, hidden_query, mask_pass, mask_query, labels, head_weight):
    groups, pass_length, part = hidden_pass.shape
    query_length = hidden_query.shape[1]
    pass_rows = groups * pass_length
    width = head_weight.shape[1]
    tokens = jnp.concatenate(
        [hidden_pass.reshape(pass_rows, part), hidden_query.reshape(groups * query_length, part)], axis=0
    )
    mask = jnp.concatenate([mask_pass.reshape(-1), mask_query.reshape(-1)]).astype(jnp.float32)
    mask = jnp.broadcast_to(mask[:, None], (mask.shape[0], 128))
    found = line_gather(tokens, n_vocab)
    pieces, at = head_pieces(head_weight, n_rows)
    all_labels = lax.all_gather(labels, "rows", axis=0, tiled=True)

    early = len(pieces) * 3 // 4
    logits = forward(found, pieces[:early], at[:early], n_vocab)
    slopes, totals_pass, totals_query, sparse_pass, sparse_query = forward(
        found,
        pieces[early:],
        at[early:],
        n_vocab,
        start=logits,
        mask=mask,
        groups=groups,
        pass_rows=pass_rows,
    )
    all_pass = lax.all_gather(sparse_pass, "rows", axis=0, tiled=True)
    all_query = lax.all_gather(sparse_query, "rows", axis=0, tiled=True)
    scaling = SHARPNESS * (width * n_vocab) ** (-0.5)
    scores = lax.psum(
        lax.dot_general(all_query, all_pass, (((1,), (1,)), ((), ())), preferred_element_type=jnp.float32),
        "vocab",
    ) * scaling
    onehot = (all_labels[:, None] == jnp.arange(all_pass.shape[0], dtype=jnp.int32)[None, :]).astype(jnp.float32)
    positive = jnp.sum(scores * onehot, axis=1, keepdims=True)
    weights = jax.nn.sigmoid(MARGIN + scores - positive) * (1.0 - onehot)
    score_grad = ((weights - onehot * jnp.sum(weights, axis=1, keepdims=True)) * scaling).astype(jnp.bfloat16)
    row = lax.axis_index("rows")
    own = (
        jnp.arange(groups, dtype=jnp.int32)[:, None] + row * groups
        == jnp.arange(all_pass.shape[0], dtype=jnp.int32)[None, :]
    ).astype(jnp.bfloat16)
    of_query = jnp.dot(own, score_grad, preferred_element_type=jnp.float32).astype(jnp.bfloat16)
    of_pass = lax.dot_general(
        own, score_grad, (((1,), (1,)), ((), ())), preferred_element_type=jnp.float32
    ).astype(jnp.bfloat16)
    query_grad = jnp.dot(of_query, all_pass, preferred_element_type=jnp.float32)
    pass_grad = jnp.dot(of_pass, all_query, preferred_element_type=jnp.float32)

    def factor(grad, totals, length):
        root = jnp.sqrt(jnp.sqrt(totals + 1.0))
        value = grad / (root * root * root)
        return jnp.broadcast_to(value[:, None, :], (groups, length, width)).reshape(groups * length, width)

    logit_grad = jnp.concatenate(
        [
            (factor(pass_grad, totals_pass, pass_length) * slopes[:pass_rows].astype(jnp.float32)).astype(jnp.bfloat16),
            (factor(query_grad, totals_query, query_length) * slopes[pass_rows:].astype(jnp.float32)).astype(jnp.bfloat16),
        ],
        axis=0,
    )
    share = n_rows // n_vocab
    place = jnp.zeros((n_rows,), jnp.int32).at[jnp.stack(at)].set(jnp.arange(n_rows, dtype=jnp.int32))

    def partial_of(block):
        order = lax.dynamic_slice(place, (block * share,), (share,))
        result = backward(logit_grad, pieces, order)
        return [result[i] for i in range(share)]

    summed = line_reduce_scatter(partial_of, n_vocab)
    summed = jnp.concatenate(summed, axis=1).astype(jnp.bfloat16)
    return (
        summed[:pass_rows].reshape(groups, pass_length, part),
        summed[pass_rows:].reshape(groups, query_length, part),
    )


def solution(mesh):
    return jax.shard_map(
        functools.partial(shards, mesh.shape["vocab"], mesh.shape["rows"]),
        mesh=mesh,
        in_specs=(
            P("rows", None, "vocab"),
            P("rows", None, "vocab"),
            P("rows", None),
            P("rows", None),
            P("rows"),
            P("rows", "vocab"),
        ),
        out_specs=(P("rows", None, "vocab"), P("rows", None, "vocab")),
        check_vma=False,
    )
```

```python
import functools

import jax
import jax.numpy as jnp
from jax import lax
from jax.experimental import pallas as pl
from jax.experimental.pallas import tpu as pltpu
from jax.sharding import PartitionSpec as P


MARGIN = 1.0
SHARPNESS = 16.0

CORES = 2


def chip_grid(n_rows):
    chips = n_rows // CORES
    tall = 1
    while (tall * 2) ** 2 <= chips and chips % (tall * 2) == 0:
        tall *= 2
    return tall, chips // tall


def line_gather(block, n):
    found = {0: block}
    left = right = block
    for step in range(1, n):
        left = lax.ppermute(left, "vocab", [(z, z - 1) for z in range(1, n - step + 1)])
        right = lax.ppermute(right, "vocab", [(z, z + 1) for z in range(step - 1, n - 1)])
        found[step] = left
        found[-step] = right
    return found


def two_paths(n_rows, n_vocab):
    return chip_grid(n_rows) == (2, 2) and n_rows == CORES * n_vocab


def row_gather(block, n_rows, n_vocab):
    if not two_paths(n_rows, n_vocab):
        whole = lax.all_gather(block, "rows", axis=0)
        return [whole[r] for r in range(n_rows)]
    x_bit, y_bit = CORES, CORES * 2
    main = [(r, r ^ (x_bit if r % CORES == 0 else y_bit)) for r in range(n_rows)]
    side = [(r, r ^ (y_bit if r % CORES == 0 else x_bit)) for r in range(n_rows)]
    twin = [(r, r ^ 1) for r in range(n_rows)]

    def move(value, pairs):
        return lax.ppermute(value, "rows", pairs)

    by_main = move(block, main)
    by_side = move(block, side)
    own_twin = move(block, twin)
    far = move(by_side, main)
    main_twin = move(by_main, twin)
    side_twin = move(by_side, twin)
    far_twin = move(far, twin)
    return [block, own_twin, by_main, side_twin, by_side, main_twin, far, far_twin]


def row_order(r, n_rows, n_vocab):
    if not two_paths(n_rows, n_vocab):
        return list(range(n_rows))
    x_bit, y_bit = CORES, CORES * 2
    along, across = (x_bit, y_bit) if r % CORES == 0 else (y_bit, x_bit)
    return [r ^ hop ^ core for hop in (0, along, across, x_bit | y_bit) for core in (0, 1)]


class Plan:
    def __init__(self, n_vocab, n_rows, depth):
        share = n_rows // n_vocab
        self.at, self.table = {}, []
        for z in range(n_vocab):
            for r in range(n_rows):
                lists = {}
                order = row_order(r, n_rows, n_vocab)
                lists["order"] = order
                early = n_rows * 3 // 4
                if two_paths(n_rows, n_vocab):
                    late = [i for i in range(3) if abs(order[2 * i] // share - z) == n_vocab - 1]
                    wait = late[0] if late else 2
                    rest = [i for i in range(3) if i != wait]
                    picks = {
                        "soon": [2 * i + core for i in rest for core in range(2)],
                        "then": [2 * wait, 2 * wait + 1],
                    }
                else:
                    picks = {"soon": list(range(early))}
                picks["last"] = list(range(early, n_rows))
                for name, pick in picks.items():
                    lists[name] = (
                        pick
                        + [order[i] // share - z for i in pick]
                        + [order[i] % share * depth for i in pick]
                    )
                place = {row: i for i, row in enumerate(order)}
                for i in range(share):
                    of = lambda block: place[block % n_vocab * share + i]
                    for step in range(1, n_vocab):
                        if 2 * step <= n_vocab:
                            units = [z + step if z + step >= n_vocab else z - step]
                        else:
                            units = [z + step, z - step]
                        lists[f"part{step}_{i}"] = [of(block) for block in units]
                    lists[f"own_{i}"] = [of(z)]
                row = []
                for name, values in lists.items():
                    self.at[name] = len(row)
                    row += values
                self.table.append(row)
        self.n_rows = n_rows

    def row(self):
        index = lax.axis_index("vocab") * self.n_rows + lax.axis_index("rows")
        table = jnp.array(self.table, jnp.int32)
        return lax.dynamic_slice(table, (index, 0), (1, table.shape[1]))[0]


def pooled(x, groups):
    length = x.shape[0] // groups
    u = 1.0 + x
    inverse = 1.0 / u
    act = jnp.log(u) + (x - (u - 1.0)) * inverse
    square = act * act
    total = jnp.sum((square * square).reshape(groups, length, -1), axis=1)
    return total, square * act * inverse


def forward_kernel(spec, plan_ref, *refs):
    at, skip, count, codes, n_pieces, depth, tile, has_total, final, groups, pass_rows = spec
    refs = list(refs)
    sources = [(code, refs.pop(0)) for code in codes]
    pieces = [refs.pop(0) for _ in range(n_pieces)]
    start_ref = refs.pop(0) if has_total else None
    mask_ref = refs.pop(0) if final else None
    if final:
        slope_ref, total_ref, sparse_ref = [refs.pop(0) for _ in range(3)]
    else:
        out_ref = refs.pop(0)
    held, weights, held_sem, weight_sem = refs
    step = pl.program_id(0)

    def weight_copy(j, t, which, slot):
        return pltpu.make_async_copy(
            pieces[which].at[:, pl.ds(pl.multiple_of(j * tile, tile), tile)],
            weights.at[slot, t],
            weight_sem.at[slot, t],
        )

    def fetch(j, slot):
        for t in range(count):
            for which in range(n_pieces):
                pl.when(plan_ref[at + t] == which + skip)(weight_copy(j, t, which, slot).start)

    def hidden_copy(t, ref):
        return pltpu.make_async_copy(
            ref.at[:, pl.ds(pl.multiple_of(plan_ref[at + 2 * count + t], 128), depth)], held.at[t], held_sem.at[t]
        )

    @pl.when(step == 0)
    def _():
        fetch(0, 0)
        for t in range(count):
            for code, ref in sources:
                pl.when(plan_ref[at + count + t] == code)(hidden_copy(t, ref).start)

    slot = lax.rem(step, 2)

    @pl.when(step + 1 < pl.num_programs(0))
    def _():
        fetch(step + 1, 1 - slot)

    @pl.when(step == 0)
    def _():
        for t in range(count):
            hidden_copy(t, sources[0][1]).wait()

    for t in range(count):
        weight_copy(step, t, 0, slot).wait()
    value = start_ref[...] if has_total else None
    for t in range(count):
        term = jnp.dot(held[t], weights[slot, t], preferred_element_type=jnp.float32)
        value = term if value is None else value + term
    if not final:
        out_ref[...] = value
        return
    mask = mask_ref[...]
    mask = jnp.concatenate([mask] * (tile // mask.shape[1]), axis=1)
    x = jnp.maximum(value, 0.0) * mask
    totals = []
    for lower, upper in ((0, pass_rows), (pass_rows, x.shape[0])):
        total, slope = pooled(x[lower:upper], groups)
        slope_ref[lower:upper, :] = slope.astype(slope_ref.dtype)
        totals.append(total)
    total = jnp.concatenate(totals, axis=0)
    total_ref[...] = total
    sparse_ref[...] = (jnp.sqrt(jnp.sqrt(total + 1.0)) - 1.0).astype(sparse_ref.dtype)


def forward(found, pieces, plan, at, count, skip=0, start=None, mask=None, groups=0, pass_rows=0, tile=512):
    rows = found[0].shape[0]
    depth, width = pieces[0].shape
    keys = sorted(found)
    final = mask is not None
    anywhere = pl.BlockSpec(memory_space=pl.ANY)
    column = lambda height: pl.BlockSpec((height, tile), lambda j, *_: (0, j))
    operands = [found[key] for key in keys] + list(pieces)
    in_specs = [anywhere] * len(operands)
    if start is not None:
        operands.append(start)
        in_specs.append(column(rows))
    if final:
        operands.append(mask)
        in_specs.append(pl.BlockSpec(mask.shape, lambda j, *_: (0, 0)))
        out_shape = [
            jax.ShapeDtypeStruct((rows, width), jnp.bfloat16),
            jax.ShapeDtypeStruct((2 * groups, width), jnp.float32),
            jax.ShapeDtypeStruct((2 * groups, width), jnp.bfloat16),
        ]
        out_specs = [column(rows), column(2 * groups), column(2 * groups)]
    else:
        out_shape = jax.ShapeDtypeStruct((rows, width), jnp.float32)
        out_specs = column(rows)
    spec = (at, skip, count, tuple(keys), len(pieces), depth, tile, start is not None, final, groups, pass_rows)
    return pl.pallas_call(
        functools.partial(forward_kernel, spec),
        out_shape=out_shape,
        grid_spec=pltpu.PrefetchScalarGridSpec(
            num_scalar_prefetch=1,
            grid=(width // tile,),
            in_specs=in_specs,
            out_specs=out_specs,
            scratch_shapes=[
                pltpu.VMEM((count, rows, depth), jnp.bfloat16),
                pltpu.VMEM((2, count, depth, tile), jnp.bfloat16),
                pltpu.SemaphoreType.DMA((count,)),
                pltpu.SemaphoreType.DMA((2, count)),
            ],
        ),
        compiler_params=pltpu.CompilerParams(
            dimension_semantics=("arbitrary",), vmem_limit_bytes=50 * 1024 * 1024
        ),
        cost_estimate=pl.CostEstimate(
            flops=2 * rows * depth * count * width,
            bytes_accessed=count * depth * width * 2 + rows * width * 8,
            transcendentals=rows * width if final else 0,
        ),
        name="forward_final" if final else "forward_part",
    )(plan, *operands)


def first_kernel(spec, plan_ref, slope_ref, pass_ref, query_ref, *refs):
    at, count, groups, pass_length, query_length = spec
    pieces, (grad_ref, out_ref, held, total, sem) = refs[:count], refs[count:]
    step = pl.program_id(0)
    tile = slope_ref.shape[1]
    steps = held.shape[0]

    def copy(j, which):
        return pltpu.make_async_copy(pieces[which].at[:, pl.ds(j * tile, tile)], held.at[j], sem.at[j])

    @pl.when(step == 0)
    def _():
        for which in range(count):

            @pl.when(plan_ref[at] == which)
            def _():
                for j in range(steps):
                    copy(j, which).start()

        total[...] = jnp.zeros_like(total)

    lower = 0
    for factor_ref, length in ((pass_ref, pass_length), (query_ref, query_length)):
        for p in range(groups):
            rows = pl.ds(lower, length)
            grad_ref[rows, :] = (slope_ref[rows, :].astype(jnp.float32) * factor_ref[p : p + 1, :]).astype(grad_ref.dtype)
            lower += length
    pltpu.make_async_copy(pieces[0].at[:, pl.ds(0, tile)], held.at[step], sem.at[step]).wait()
    total[...] += lax.dot_general(
        grad_ref[...], held[step], (((1,), (1,)), ((), ())), preferred_element_type=jnp.float32
    )

    @pl.when(step == steps - 1)
    def _():
        out_ref[...] = total[...].astype(out_ref.dtype)


def backward_first(slopes, factor_pass, factor_query, lengths, pieces, plan, at, tile=512):
    rows, width = slopes.shape
    groups = factor_pass.shape[0]
    depth = pieces[0].shape[0]
    count = len(pieces)
    column = lambda height: pl.BlockSpec((height, tile), lambda j, *_: (0, j))
    return pl.pallas_call(
        functools.partial(first_kernel, (at, count, groups) + lengths),
        out_shape=[
            jax.ShapeDtypeStruct((rows, width), jnp.bfloat16),
            jax.ShapeDtypeStruct((rows, depth), jnp.bfloat16),
        ],
        grid_spec=pltpu.PrefetchScalarGridSpec(
            num_scalar_prefetch=1,
            grid=(width // tile,),
            in_specs=[column(rows), column(groups), column(groups)]
            + [pl.BlockSpec(memory_space=pl.ANY)] * count,
            out_specs=[column(rows), pl.BlockSpec((rows, depth), lambda j, *_: (0, 0))],
            scratch_shapes=[
                pltpu.VMEM((width // tile, depth, tile), jnp.bfloat16),
                pltpu.VMEM((rows, depth), jnp.float32),
                pltpu.SemaphoreType.DMA((width // tile,)),
            ],
        ),
        compiler_params=pltpu.CompilerParams(
            dimension_semantics=("arbitrary",), vmem_limit_bytes=50 * 1024 * 1024
        ),
        cost_estimate=pl.CostEstimate(
            flops=2 * rows * depth * width,
            bytes_accessed=(depth * width + 2 * rows * width + rows * depth) * 2,
            transcendentals=0,
        ),
        name="backward_first",
    )(plan, slopes, factor_pass, factor_query, *pieces)


def backward_kernel(spec, plan_ref, slopes_ref, *refs):
    at_plan, count, parts, adds = spec
    units = len(adds)
    n_adds = max([0] + [i + 1 for unit in adds for i in unit])
    pieces, refs = refs[:count], refs[count:]
    running, refs = refs[:n_adds], refs[n_adds:]
    outs, (held, slopes, piece_sem, slope_sem) = refs[:units], refs[units:]
    rows = slopes_ref.shape[0] // parts

    def slope_copy(i):
        at = pl.ds(pl.multiple_of(i * rows, 16), rows)
        return pltpu.make_async_copy(slopes_ref.at[at, :], slopes.at[at, :], slope_sem.at[i])

    for unit in range(units):
        for which in range(count):
            copy = pltpu.make_async_copy(pieces[which], held.at[unit], piece_sem.at[unit])
            pl.when(plan_ref[at_plan + unit] == which)(copy.start)
        if unit == 0:
            for i in range(parts):
                slope_copy(i).start()
    for unit in range(units):
        pltpu.make_async_copy(pieces[0], held.at[unit], piece_sem.at[unit]).wait()

        @pl.loop(0, parts)
        def _(i):
            if unit == 0:
                slope_copy(i).wait()
            at = pl.ds(pl.multiple_of(i * rows, 16), rows)
            value = lax.dot_general(
                slopes[at, :], held[unit], (((1,), (1,)), ((), ())), preferred_element_type=jnp.float32
            ).astype(jnp.bfloat16)
            if adds[unit]:
                value = value.astype(jnp.float32)
                for j in adds[unit]:
                    value = value + running[j][at, :].astype(jnp.float32)
            outs[unit][at, :] = value.astype(outs[unit].dtype)


def backward(slopes, pieces, plan, at, running=(), adds=((),)):
    rows, width = slopes.shape
    depth = pieces[0].shape[0]
    count, units = len(pieces), len(adds)
    parts = 3 if rows % 48 == 0 else 1
    whole = pl.BlockSpec(memory_space=pltpu.VMEM)
    anywhere = pl.BlockSpec(memory_space=pl.ANY)
    return pl.pallas_call(
        functools.partial(backward_kernel, (at, count, parts, adds)),
        out_shape=[jax.ShapeDtypeStruct((rows, depth), jnp.bfloat16)] * units,
        in_specs=[pl.BlockSpec(memory_space=pltpu.SMEM)] + [anywhere] * (1 + count) + [whole] * len(running),
        out_specs=[whole] * units,
        scratch_shapes=[
            pltpu.VMEM((units, depth, width), jnp.bfloat16),
            pltpu.VMEM((rows, width), jnp.bfloat16),
            pltpu.SemaphoreType.DMA((units,)),
            pltpu.SemaphoreType.DMA((parts,)),
        ],
        compiler_params=pltpu.CompilerParams(vmem_limit_bytes=50 * 1024 * 1024),
        cost_estimate=pl.CostEstimate(
            flops=2 * rows * depth * units * width,
            bytes_accessed=(units * depth * width + rows * width + units * rows * depth) * 2,
            transcendentals=0,
        ),
        name="backward_part",
    )(plan, slopes, *pieces, *running)


def line_reduce_scatter(first, product, n, share):
    left, right = [None] * share, [None] * share
    for step in range(1, n):
        for i in range(share):
            name = f"part{step}_{i}"
            if step == 1 and i == 0:
                to_left = to_right = first
            elif 2 * step <= n:
                running = () if step == 1 else (left[i], right[i])
                (to_left,) = product(name, running, (tuple(range(len(running))),))
                to_right = to_left
            else:
                to_left, to_right = product(name, (left[i], right[i]), ((0,), (1,)))
            left[i] = lax.ppermute(to_left, "vocab", [(d, d - 1) for d in range(n - step, n)])
            right[i] = lax.ppermute(to_right, "vocab", [(d, d + 1) for d in range(step)])
    terms = []
    for i in range(share):
        own = product(f"own_{i}", (), ((),))[0]
        terms.append(own.astype(jnp.float32) + left[i].astype(jnp.float32) + right[i].astype(jnp.float32))
    return terms


def shards(n_vocab, n_rows, *arguments):
    return body(n_vocab, n_rows, *arguments)


def body(n_vocab, n_rows, hidden_pass, hidden_query, mask_pass, mask_query, labels, head_weight):
    groups, pass_length, part = hidden_pass.shape
    query_length = hidden_query.shape[1]
    pass_rows = groups * pass_length
    depth, width = head_weight.shape
    share = n_rows // n_vocab
    plans = Plan(n_vocab, n_rows, depth)
    plan = plans.row()
    order = plan[plans.at["order"] : plans.at["order"] + n_rows]
    tokens = jnp.concatenate(
        [hidden_pass.reshape(pass_rows, part), hidden_query.reshape(groups * query_length, part)], axis=0
    )
    mask = jnp.concatenate([mask_pass.reshape(-1), mask_query.reshape(-1)]).astype(jnp.float32)
    mask = jnp.broadcast_to(mask[:, None], (mask.shape[0], 128))
    found = line_gather(tokens, n_vocab)
    pieces = row_gather(head_weight, n_rows, n_vocab)
    all_labels = lax.all_gather(labels, "rows", axis=0)[order].reshape(-1)
    passages = (order[:, None] * groups + jnp.arange(groups, dtype=jnp.int32)[None, :]).reshape(-1)
    onehot = (all_labels[:, None] == passages[None, :]).astype(jnp.float32)

    early = n_rows * 3 // 4
    if two_paths(n_rows, n_vocab):
        near = {code: block for code, block in found.items() if abs(code) < n_vocab - 1}
        logits = forward(near, pieces[:early], plan, plans.at["soon"], 4)
        logits = forward(found, pieces[:early], plan, plans.at["then"], 2, start=logits)
    else:
        logits = forward(found, pieces[:early], plan, plans.at["soon"], early)
    slopes, totals, sparse = forward(
        found,
        pieces[early:],
        plan,
        plans.at["last"],
        n_rows - early,
        skip=early,
        start=logits,
        mask=mask,
        groups=groups,
        pass_rows=pass_rows,
    )
    all_sparse = jnp.stack(row_gather(sparse, n_rows, n_vocab))
    all_pass = all_sparse[:, :groups].reshape(-1, width)
    all_query = all_sparse[:, groups:].reshape(-1, width)
    scaling = SHARPNESS * (width * n_vocab) ** (-0.5)
    scores = lax.dot_general(all_query, all_pass, (((1,), (1,)), ((), ())), preferred_element_type=jnp.float32)
    shifted = [
        lax.ppermute(scores, "vocab", [(d, (d + s) % n_vocab) for d in range(n_vocab)]) for s in range(1, n_vocab)
    ]
    for other in shifted:
        scores = scores + other
    scores = scores * scaling
    positive = jnp.sum(scores * onehot, axis=1, keepdims=True)
    weights = jax.nn.sigmoid(MARGIN + scores - positive) * (1.0 - onehot)
    score_grad = ((weights - onehot * jnp.sum(weights, axis=1, keepdims=True)) * scaling).astype(jnp.bfloat16)
    if two_paths(n_rows, n_vocab):
        of_query, of_pass = score_grad[:groups], score_grad[:, :groups]
    else:
        row = lax.axis_index("rows") * groups
        of_query = lax.dynamic_slice_in_dim(score_grad, row, groups, 0)
        of_pass = lax.dynamic_slice_in_dim(score_grad, row, groups, 1)
    query_grad = jnp.dot(of_query, all_pass, preferred_element_type=jnp.float32)
    pass_grad = lax.dot_general(of_pass, all_query, (((0,), (0,)), ((), ())), preferred_element_type=jnp.float32)
    root = jnp.sqrt(jnp.sqrt(totals + 1.0))
    cube = root * root * root
    logit_grad, first = backward_first(
        slopes,
        pass_grad / cube[:groups],
        query_grad / cube[groups:],
        (pass_length, query_length),
        pieces,
        plan,
        plans.at["part1_0"],
    )

    def product(name, running, adds):
        return backward(logit_grad, pieces, plan, plans.at[name], running, adds)

    summed = line_reduce_scatter(first, product, n_vocab, share)
    summed = jnp.concatenate(summed, axis=1).astype(jnp.bfloat16)
    return (
        summed[:pass_rows].reshape(groups, pass_length, part),
        summed[pass_rows:].reshape(groups, query_length, part),
    )


def solution(mesh):
    n_vocab, n_rows = mesh.shape["vocab"], mesh.shape["rows"]
    return jax.shard_map(
        functools.partial(shards, n_vocab, n_rows),
        mesh=mesh,
        in_specs=(
            P("rows", None, "vocab"),
            P("rows", None, "vocab"),
            P("rows", None),
            P("rows", None),
            P("rows"),
            P("rows", "vocab"),
        ),
        out_specs=(P("rows", None, "vocab"), P("rows", None, "vocab")),
        check_vma=False,
    )
```

```python
import functools

import jax
import jax.numpy as jnp
from jax import lax
from jax.experimental import pallas as pl
from jax.experimental.pallas import tpu as pltpu
from jax.sharding import PartitionSpec as P


MARGIN = 1.0
SHARPNESS = 16.0

VMEM_BYTES = 62 * 1024 * 1024
CORES = 2


def chip_grid(n_rows):
    chips = n_rows // CORES
    tall = 1
    while (tall * 2) ** 2 <= chips and chips % (tall * 2) == 0:
        tall *= 2
    return tall, chips // tall


def line_gather(block, n):
    found = {0: block}
    left = right = block
    for step in range(1, n):
        left = lax.ppermute(left, "vocab", [(z, z - 1) for z in range(1, n - step + 1)])
        right = lax.ppermute(right, "vocab", [(z, z + 1) for z in range(step - 1, n - 1)])
        found[step] = left
        found[-step] = right
    return found


def two_paths(n_rows, n_vocab):
    return chip_grid(n_rows) == (2, 2) and n_rows == CORES * n_vocab


def row_gather(block, n_rows, n_vocab):
    if not two_paths(n_rows, n_vocab):
        whole = lax.all_gather(block, "rows", axis=0)
        return [whole[r] for r in range(n_rows)]
    x_bit, y_bit = CORES, CORES * 2
    main = [(r, r ^ (x_bit if r % CORES == 0 else y_bit)) for r in range(n_rows)]
    side = [(r, r ^ (y_bit if r % CORES == 0 else x_bit)) for r in range(n_rows)]
    twin = [(r, r ^ 1) for r in range(n_rows)]

    def move(value, pairs):
        return lax.ppermute(value, "rows", pairs)

    by_main = move(block, main)
    by_side = move(block, side)
    own_twin = move(block, twin)
    far = move(by_side, main)
    main_twin = move(by_main, twin)
    side_twin = move(by_side, twin)
    far_twin = move(far, twin)
    return [block, own_twin, by_main, side_twin, by_side, main_twin, far, far_twin]


def row_order(r, n_rows, n_vocab):
    if not two_paths(n_rows, n_vocab):
        return list(range(n_rows))
    x_bit, y_bit = CORES, CORES * 2
    along, across = (x_bit, y_bit) if r % CORES == 0 else (y_bit, x_bit)
    return [r ^ hop ^ core for hop in (0, along, across, x_bit | y_bit) for core in (0, 1)]


class Plan:
    def __init__(self, n_vocab, n_rows, depth):
        share = n_rows // n_vocab
        self.at, self.table = {}, []
        for z in range(n_vocab):
            for r in range(n_rows):
                lists = {}
                order = row_order(r, n_rows, n_vocab)
                lists["order"] = order
                half = n_rows // 2
                picks = {"soon": list(range(half)), "last": list(range(half, n_rows))}
                if two_paths(n_rows, n_vocab):
                    late = [i for i in range(3) if abs(order[2 * i] // share - z) == n_vocab - 1]
                    wait = late[0] if late else 2
                    rest = [i for i in range(4) if i != wait]
                    rest = rest[:2] + [wait, rest[2]]
                    pick = [2 * i + core for i in rest for core in range(2)]
                    picks = {"soon": pick[:half], "last": pick[half:]}
                for name, pick in picks.items():
                    lists[name] = (
                        pick
                        + [order[i] // share - z for i in pick]
                        + [order[i] % share * depth for i in pick]
                    )
                place = {row: i for i, row in enumerate(order)}
                for i in range(share):
                    of = lambda block: place[block % n_vocab * share + i]
                    for step in range(1, n_vocab):
                        if 2 * step <= n_vocab:
                            units = [z + step if z + step >= n_vocab else z - step]
                        else:
                            units = [z + step, z - step]
                        lists[f"part{step}_{i}"] = [of(block) for block in units]
                    lists[f"own_{i}"] = [of(z)]
                row = []
                for name, values in lists.items():
                    self.at[name] = len(row)
                    row += values
                self.table.append(row)
        self.n_rows = n_rows

    def row(self):
        index = lax.axis_index("vocab") * self.n_rows + lax.axis_index("rows")
        table = jnp.array(self.table, jnp.int32)
        return lax.dynamic_slice(table, (index, 0), (1, table.shape[1]))[0]


def pooled(x, groups):
    length = x.shape[0] // groups
    u = 1.0 + x
    inverse = 1.0 / u
    act = jnp.log(u) + (x - (u - 1.0)) * inverse
    square = act * act
    total = jnp.sum((square * square).reshape(groups, length, -1), axis=1)
    return total, square * act * inverse


def forward_kernel(spec, plan_ref, *refs):
    at, count, codes, n_pieces, depth, tile, final, groups, pass_rows, kept = spec
    refs = list(refs)
    sources = [(code, refs.pop(0)) for code in codes]
    pieces = [refs.pop(0) for _ in range(n_pieces)]
    if final:
        start_ref, mask_ref = refs.pop(0), refs.pop(0)
        del refs[:kept]
        slope_ref, total_ref, sparse_ref = [refs.pop(0) for _ in range(3)]
    else:
        out_ref = refs.pop(0)
    held, weights, held_sem, weight_sem = refs
    step = pl.program_id(0)

    def weight_copy(j, t, which, slot):
        return pltpu.make_async_copy(
            pieces[which].at[:, pl.ds(pl.multiple_of(j * tile, tile), tile)],
            weights.at[slot, pl.ds(t * depth, depth)],
            weight_sem.at[slot, t],
        )

    def fetch(j, slot):
        for t in range(count):
            for which in range(n_pieces):
                pl.when(plan_ref[at + t] == which)(weight_copy(j, t, which, slot).start)

    def hidden_copy(t, ref):
        return pltpu.make_async_copy(
            ref.at[:, pl.ds(pl.multiple_of(plan_ref[at + 2 * count + t], 128), depth)],
            held.at[:, pl.ds(t * depth, depth)],
            held_sem.at[t],
        )

    @pl.when(step == 0)
    def _():
        fetch(0, 0)
        for t in range(count):
            for code, ref in sources:
                pl.when(plan_ref[at + count + t] == code)(hidden_copy(t, ref).start)

    slot = lax.rem(step, 2)

    @pl.when(step + 1 < pl.num_programs(0))
    def _():
        fetch(step + 1, 1 - slot)

    @pl.when(step == 0)
    def _():
        for t in range(count):
            hidden_copy(t, sources[0][1]).wait()

    for t in range(count):
        weight_copy(step, t, 0, slot).wait()
    value = jnp.dot(held[...], weights[slot], preferred_element_type=jnp.float32)
    if not final:
        out_ref[...] = value
        return
    mask = mask_ref[...]
    mask = jnp.concatenate([mask] * (tile // mask.shape[1]), axis=1)
    x = jnp.maximum(value + start_ref[...], 0.0) * mask
    totals = []
    for lower, upper in ((0, pass_rows), (pass_rows, x.shape[0])):
        total, slope = pooled(x[lower:upper], groups)
        slope_ref[lower:upper, :] = slope.astype(slope_ref.dtype)
        totals.append(total)
    total = jnp.concatenate(totals, axis=0)
    total_ref[...] = total
    sparse_ref[...] = (jnp.sqrt(jnp.sqrt(total + 1.0)) - 1.0).astype(sparse_ref.dtype)


def forward(found, pieces, plan, at, count, tile=512, pool=None):
    rows = found[0].shape[0]
    depth, width = pieces[0].shape
    keys = sorted(found)
    anywhere = pl.BlockSpec(memory_space=pl.ANY)
    operands = [found[key] for key in keys] + list(pieces)
    in_specs = [anywhere] * len(operands)
    groups = pass_rows = 0
    filled = ()
    if pool is not None:
        start, mask, groups, pass_rows, whole, first, filled = pool
        skip = first // tile
        column = lambda height: pl.BlockSpec((height, tile), lambda j, *_: (0, j + skip))
        operands += [start, mask]
        in_specs.append(pl.BlockSpec((rows, tile), lambda j, *_: (0, j)))
        in_specs.append(pl.BlockSpec(mask.shape, lambda j, *_: (0, 0)))
        in_specs += [anywhere] * len(filled)
        out_shape = [
            jax.ShapeDtypeStruct((rows, whole), jnp.bfloat16),
            jax.ShapeDtypeStruct((2 * groups, whole), jnp.float32),
            jax.ShapeDtypeStruct((2 * groups, whole), jnp.bfloat16),
        ]
        out_specs = [column(rows), column(2 * groups), column(2 * groups)]
    else:
        out_shape = jax.ShapeDtypeStruct((rows, width), jnp.float32)
        out_specs = pl.BlockSpec((rows, tile), lambda j, *_: (0, j))
    spec = (at, count, tuple(keys), len(pieces), depth, tile, pool is not None, groups, pass_rows, len(filled))
    return pl.pallas_call(
        functools.partial(forward_kernel, spec),
        out_shape=out_shape,
        grid_spec=pltpu.PrefetchScalarGridSpec(
            num_scalar_prefetch=1,
            grid=(width // tile,),
            in_specs=in_specs,
            out_specs=out_specs,
            scratch_shapes=[
                pltpu.VMEM((rows, count * depth), jnp.bfloat16),
                pltpu.VMEM((2, count * depth, tile), jnp.bfloat16),
                pltpu.SemaphoreType.DMA((count,)),
                pltpu.SemaphoreType.DMA((2, count)),
            ],
        ),
        input_output_aliases={1 + len(operands) + i: i for i in range(len(filled))},
        compiler_params=pltpu.CompilerParams(
            dimension_semantics=("arbitrary",), vmem_limit_bytes=VMEM_BYTES
        ),
        cost_estimate=pl.CostEstimate(
            flops=2 * rows * depth * count * width,
            bytes_accessed=count * depth * width * 2 + rows * width * 8,
            transcendentals=rows * width if pool is not None else 0,
        ),
        name="forward_part" if pool is None else "forward_final",
    )(plan, *operands, *filled)


def spans(parts):
    found, lower = [], 0
    for part in parts:
        found.append((lower, part[0].shape[1]))
        lower += part[0].shape[1]
    return found


def first_kernel(spec, plan_ref, slope_ref, pass_ref, query_ref, *refs):
    at, count, ranges, groups, pass_length, query_length, keep = spec
    parts = [refs[i * count : (i + 1) * count] for i in range(len(ranges))]
    refs = refs[count * len(ranges) :]
    (grad_ref, out_ref) = refs[:2] if keep else (refs[1], refs[0])
    held, total, sem = refs[2:]
    step = pl.program_id(0)
    tile = slope_ref.shape[1]
    steps = held.shape[0]

    def copy(j, which):
        i = [i for i, (lower, width) in enumerate(ranges) if lower <= j * tile < lower + width][0]
        return pltpu.make_async_copy(
            parts[i][which].at[:, pl.ds(j * tile - ranges[i][0], tile)], held.at[j], sem.at[j]
        )

    @pl.when(step == 0)
    def _():
        for which in range(count):

            @pl.when(plan_ref[at] == which)
            def _():
                for j in range(steps):
                    copy(j, which).start()

        total[...] = jnp.zeros_like(total)

    lower = 0
    for factor_ref, length in ((pass_ref, pass_length), (query_ref, query_length)):
        for p in range(groups):
            rows = pl.ds(lower, length)
            grad_ref[rows, :] = (slope_ref[rows, :].astype(jnp.float32) * factor_ref[p : p + 1, :]).astype(grad_ref.dtype)
            lower += length
    pltpu.make_async_copy(parts[0][0].at[:, pl.ds(0, tile)], held.at[step], sem.at[step]).wait()
    total[...] += lax.dot_general(
        grad_ref[...], held[step], (((1,), (1,)), ((), ())), preferred_element_type=jnp.float32
    )

    @pl.when(step == steps - 1)
    def _():
        out_ref[...] = total[...].astype(out_ref.dtype)


def backward_first(slopes, factor_pass, factor_query, lengths, parts, plan, at, keep, tile=1024):
    rows, width = slopes.shape
    groups = factor_pass.shape[0]
    depth = parts[0][0].shape[0]
    count = len(parts[0])
    pieces = [piece for part in parts for piece in part]
    column = lambda height: pl.BlockSpec((height, tile), lambda j, *_: (0, j))
    out_shape = [jax.ShapeDtypeStruct((rows, depth), jnp.bfloat16)]
    out_specs = [pl.BlockSpec((rows, depth), lambda j, *_: (0, 0))]
    scratch = [] if keep else [pltpu.VMEM((rows, tile), jnp.bfloat16)]
    if keep:
        out_shape.insert(0, jax.ShapeDtypeStruct((rows, width), jnp.bfloat16))
        out_specs.insert(0, column(rows))
    return pl.pallas_call(
        functools.partial(first_kernel, (at, count, spans(parts), groups) + lengths + (keep,)),
        out_shape=out_shape,
        grid_spec=pltpu.PrefetchScalarGridSpec(
            num_scalar_prefetch=1,
            grid=(width // tile,),
            in_specs=[column(rows), column(groups), column(groups)]
            + [pl.BlockSpec(memory_space=pl.ANY)] * len(pieces),
            out_specs=out_specs,
            scratch_shapes=scratch
            + [
                pltpu.VMEM((width // tile, depth, tile), jnp.bfloat16),
                pltpu.VMEM((rows, depth), jnp.float32),
                pltpu.SemaphoreType.DMA((width // tile,)),
            ],
        ),
        compiler_params=pltpu.CompilerParams(
            dimension_semantics=("arbitrary",), vmem_limit_bytes=VMEM_BYTES
        ),
        cost_estimate=pl.CostEstimate(
            flops=2 * rows * depth * width,
            bytes_accessed=(depth * width + 2 * rows * width + rows * depth) * 2,
            transcendentals=0,
        ),
        name="backward_first",
    )(plan, slopes, factor_pass, factor_query, *pieces)


def backward_kernel(spec, plan_ref, slopes_ref, *refs):
    at_plan, count, ranges, parts, adds = spec
    units = len(adds)
    n_adds = max([0] + [i + 1 for unit in adds for i in unit])
    groups = [refs[i * count : (i + 1) * count] for i in range(len(ranges))]
    refs = refs[count * len(ranges) :]
    running, refs = refs[:n_adds], refs[n_adds:]
    outs, (held, slopes, piece_sem, slope_sem) = refs[:units], refs[units:]
    rows = slopes_ref.shape[0] // parts

    def slope_copy(i):
        at = pl.ds(pl.multiple_of(i * rows, 16), rows)
        return pltpu.make_async_copy(slopes_ref.at[at, :], slopes.at[at, :], slope_sem.at[i])

    def piece_copy(unit, i, which):
        lower, width = ranges[i]
        return pltpu.make_async_copy(
            groups[i][which], held.at[unit, :, pl.ds(lower, width)], piece_sem.at[unit, i]
        )

    for unit in range(units):
        for i in range(len(ranges)):
            for which in range(count):
                pl.when(plan_ref[at_plan + unit] == which)(piece_copy(unit, i, which).start)
        if unit == 0:
            for i in range(parts):
                slope_copy(i).start()
    for unit in range(units):
        for i in range(len(ranges)):
            piece_copy(unit, i, 0).wait()

        @pl.loop(0, parts)
        def _(i):
            if unit == 0:
                slope_copy(i).wait()
            at = pl.ds(pl.multiple_of(i * rows, 16), rows)
            value = lax.dot_general(
                slopes[at, :], held[unit], (((1,), (1,)), ((), ())), preferred_element_type=jnp.float32
            ).astype(jnp.bfloat16)
            if adds[unit]:
                value = value.astype(jnp.float32)
                for j in adds[unit]:
                    value = value + running[j][at, :].astype(jnp.float32)
            outs[unit][at, :] = value.astype(outs[unit].dtype)


def backward(slopes, groups, plan, at, running=(), adds=((),)):
    rows, width = slopes.shape
    depth = groups[0][0].shape[0]
    pieces = [piece for group in groups for piece in group]
    count, units = len(groups[0]), len(adds)
    parts = 3 if rows % 48 == 0 else 1
    whole = pl.BlockSpec(memory_space=pltpu.VMEM)
    anywhere = pl.BlockSpec(memory_space=pl.ANY)
    return pl.pallas_call(
        functools.partial(backward_kernel, (at, count, spans(groups), parts, adds)),
        out_shape=[jax.ShapeDtypeStruct((rows, depth), jnp.bfloat16)] * units,
        in_specs=[pl.BlockSpec(memory_space=pltpu.SMEM)] + [anywhere] * (1 + len(pieces)) + [whole] * len(running),
        out_specs=[whole] * units,
        scratch_shapes=[
            pltpu.VMEM((units, depth, width), jnp.bfloat16),
            pltpu.VMEM((rows, width), jnp.bfloat16),
            pltpu.SemaphoreType.DMA((units, len(groups))),
            pltpu.SemaphoreType.DMA((parts,)),
        ],
        compiler_params=pltpu.CompilerParams(vmem_limit_bytes=VMEM_BYTES),
        cost_estimate=pl.CostEstimate(
            flops=2 * rows * depth * units * width,
            bytes_accessed=(units * depth * width + rows * width + units * rows * depth) * 2,
            transcendentals=0,
        ),
        name="backward_part",
    )(plan, slopes, *pieces, *running)


def line_reduce_scatter(first, product, n, share):
    left, right = [None] * share, [None] * share
    for step in range(1, n):
        for i in range(share):
            name = f"part{step}_{i}"
            if step == 1 and i < 2:
                to_left = to_right = first(name, i)
            elif 2 * step <= n:
                running = () if step == 1 else (left[i], right[i])
                (to_left,) = product(name, running, (tuple(range(len(running))),))
                to_right = to_left
            else:
                to_left, to_right = product(name, (left[i], right[i]), ((0,), (1,)))
            left[i] = lax.ppermute(to_left, "vocab", [(d, d - 1) for d in range(n - step, n)])
            right[i] = lax.ppermute(to_right, "vocab", [(d, d + 1) for d in range(step)])
    terms = []
    for i in range(share):
        own = product(f"own_{i}", (), ((),))[0]
        terms.append(own.astype(jnp.float32) + left[i].astype(jnp.float32) + right[i].astype(jnp.float32))
    return terms


def shards(n_vocab, n_rows, *arguments):
    return body(n_vocab, n_rows, *arguments)


def body(n_vocab, n_rows, hidden_pass, hidden_query, mask_pass, mask_query, labels, head_weight):
    groups, pass_length, part = hidden_pass.shape
    query_length = hidden_query.shape[1]
    pass_rows = groups * pass_length
    depth, width = head_weight.shape
    share = n_rows // n_vocab
    plans = Plan(n_vocab, n_rows, depth)
    plan = plans.row()
    order = plan[plans.at["order"] : plans.at["order"] + n_rows]
    tokens = jnp.concatenate(
        [hidden_pass.reshape(pass_rows, part), hidden_query.reshape(groups * query_length, part)], axis=0
    )
    mask = jnp.concatenate([mask_pass.reshape(-1), mask_query.reshape(-1)]).astype(jnp.float32)
    mask = jnp.broadcast_to(mask[:, None], (mask.shape[0], 128))
    found = line_gather(tokens, n_vocab)
    halves = 2 if two_paths(n_rows, n_vocab) and width % 2048 == 0 else 1
    part_width = width // halves
    parts = []
    for i in range(halves):
        own = head_weight
        if i > 0:
            own, _ = lax.optimization_barrier((head_weight, tokens))
        own = own[:, i * part_width : (i + 1) * part_width]
        parts.append(row_gather(own, n_rows, n_vocab))
    all_labels = jnp.stack(row_gather(labels, n_rows, n_vocab)).reshape(-1)
    passages = (order[:, None] * groups + jnp.arange(groups, dtype=jnp.int32)[None, :]).reshape(-1)
    onehot = (all_labels[:, None] == passages[None, :]).astype(jnp.float32)

    half = n_rows // 2
    near, soon = found, n_rows
    if two_paths(n_rows, n_vocab):
        near = {code: block for code, block in found.items() if abs(code) < n_vocab - 1}
        soon = n_rows - 2
    logits, filled = [], ()
    for i in range(halves):
        logits.append(forward(near, parts[i][:soon], plan, plans.at["soon"], half))
    for i in range(halves):
        pool = (logits[i], mask, groups, pass_rows, width, i * part_width, filled)
        filled = forward(found, parts[i], plan, plans.at["last"], half, pool=pool)
    slopes, totals, sparse = filled
    all_sparse = jnp.stack(row_gather(sparse, n_rows, n_vocab))
    all_pass = all_sparse[:, :groups].reshape(-1, width)
    all_query = all_sparse[:, groups:].reshape(-1, width)
    scaling = SHARPNESS * (width * n_vocab) ** (-0.5)
    scores = lax.dot_general(all_query, all_pass, (((1,), (1,)), ((), ())), preferred_element_type=jnp.float32)
    shifted = [
        lax.ppermute(scores, "vocab", [(d, (d + s) % n_vocab) for d in range(n_vocab)]) for s in range(1, n_vocab)
    ]
    for other in shifted:
        scores = scores + other
    scores = scores * scaling
    positive = jnp.sum(scores * onehot, axis=1, keepdims=True)
    weights = jax.nn.sigmoid(MARGIN + scores - positive) * (1.0 - onehot)
    score_grad = ((weights - onehot * jnp.sum(weights, axis=1, keepdims=True)) * scaling).astype(jnp.bfloat16)
    if two_paths(n_rows, n_vocab):
        of_query, of_pass = score_grad[:groups], score_grad[:, :groups]
    else:
        row = lax.axis_index("rows") * groups
        of_query = lax.dynamic_slice_in_dim(score_grad, row, groups, 0)
        of_pass = lax.dynamic_slice_in_dim(score_grad, row, groups, 1)
    query_grad = jnp.dot(of_query, all_pass, preferred_element_type=jnp.float32)
    pass_grad = lax.dot_general(of_pass, all_query, (((0,), (0,)), ((), ())), preferred_element_type=jnp.float32)
    root = jnp.sqrt(jnp.sqrt(totals + 1.0))
    cube = root * root * root
    factors = (pass_grad / cube[:groups], query_grad / cube[groups:], (pass_length, query_length))
    logit_grad = []

    def first(name, i):
        keep = i == 1 or share == 1
        *grad, block = backward_first(slopes, *factors, parts, plan, plans.at[name], keep)
        logit_grad.extend(grad)
        return block

    def product(name, running, adds):
        return backward(logit_grad[0], parts, plan, plans.at[name], running, adds)

    summed = line_reduce_scatter(first, product, n_vocab, share)
    summed = jnp.concatenate(summed, axis=1).astype(jnp.bfloat16)
    return (
        summed[:pass_rows].reshape(groups, pass_length, part),
        summed[pass_rows:].reshape(groups, query_length, part),
    )


def solution(mesh):
    n_vocab, n_rows = mesh.shape["vocab"], mesh.shape["rows"]
    return jax.shard_map(
        functools.partial(shards, n_vocab, n_rows),
        mesh=mesh,
        in_specs=(
            P("rows", None, "vocab"),
            P("rows", None, "vocab"),
            P("rows", None),
            P("rows", None),
            P("rows"),
            P("rows", "vocab"),
        ),
        out_specs=(P("rows", None, "vocab"), P("rows", None, "vocab")),
        check_vma=False,
    )
```

```python
import functools

import jax
import jax.numpy as jnp
from jax import lax
from jax.experimental import pallas as pl
from jax.experimental.pallas import tpu as pltpu
from jax.sharding import PartitionSpec as P


MARGIN = 1.0
SHARPNESS = 16.0

VMEM_BYTES = 62 * 1024 * 1024
FIRST_VMEM_BYTES = 24 * 1024 * 1024
SMALL_VMEM_BYTES = 48 * 1024 * 1024
CORES = 2


def chip_grid(n_rows):
    chips = n_rows // CORES
    tall = 1
    while (tall * 2) ** 2 <= chips and chips % (tall * 2) == 0:
        tall *= 2
    return tall, chips // tall


def line_gather(block, n):
    found = {0: block}
    left = right = block
    for step in range(1, n):
        left = lax.ppermute(left, "vocab", [(z, z - 1) for z in range(1, n - step + 1)])
        right = lax.ppermute(right, "vocab", [(z, z + 1) for z in range(step - 1, n - 1)])
        found[step] = left
        found[-step] = right
    return found


def two_paths(n_rows, n_vocab):
    return chip_grid(n_rows) == (2, 2) and n_rows == CORES * n_vocab


def row_gather(block, n_rows, n_vocab):
    if not two_paths(n_rows, n_vocab):
        whole = lax.all_gather(block, "rows", axis=0)
        return [whole[r] for r in range(n_rows)]
    x_bit, y_bit = CORES, CORES * 2
    main = [(r, r ^ (x_bit if r % CORES == 0 else y_bit)) for r in range(n_rows)]
    side = [(r, r ^ (y_bit if r % CORES == 0 else x_bit)) for r in range(n_rows)]
    twin = [(r, r ^ 1) for r in range(n_rows)]

    def move(value, pairs):
        return lax.ppermute(value, "rows", pairs)

    by_main = move(block, main)
    by_side = move(block, side)
    own_twin = move(block, twin)
    far = move(by_side, main)
    main_twin = move(by_main, twin)
    side_twin = move(by_side, twin)
    far_twin = move(far, twin)
    return [block, own_twin, by_main, side_twin, by_side, main_twin, far, far_twin]


def row_order(r, n_rows, n_vocab):
    if not two_paths(n_rows, n_vocab):
        return list(range(n_rows))
    x_bit, y_bit = CORES, CORES * 2
    along, across = (x_bit, y_bit) if r % CORES == 0 else (y_bit, x_bit)
    return [r ^ hop ^ core for hop in (0, along, across, x_bit | y_bit) for core in (0, 1)]


class Plan:
    def __init__(self, n_vocab, n_rows, depth):
        share = n_rows // n_vocab
        self.at, self.table = {}, []
        for z in range(n_vocab):
            for r in range(n_rows):
                lists = {}
                order = row_order(r, n_rows, n_vocab)
                lists["order"] = order
                half = n_rows // 2
                picks = {"soon": list(range(half)), "last": list(range(half, n_rows))}
                if two_paths(n_rows, n_vocab):
                    late = [i for i in range(3) if abs(order[2 * i] // share - z) == n_vocab - 1]
                    wait = late[0] if late else 2
                    rest = [i for i in range(4) if i != wait]
                    rest = rest[:2] + [wait, rest[2]]
                    pick = [2 * i + core for i in rest for core in range(2)]
                    picks = {"soon": pick[:half], "last": pick[half:]}
                for name, pick in picks.items():
                    lists[name] = (
                        pick
                        + [order[i] // share - z for i in pick]
                        + [order[i] % share * depth for i in pick]
                    )
                place = {row: i for i, row in enumerate(order)}
                for i in range(share):
                    of = lambda block: place[block % n_vocab * share + i]
                    for step in range(1, n_vocab):
                        if 2 * step <= n_vocab:
                            units = [z + step if z + step >= n_vocab else z - step]
                        else:
                            units = [z + step, z - step]
                        lists[f"part{step}_{i}"] = [of(block) for block in units]
                    lists[f"own_{i}"] = [of(z)]
                row = []
                for name, values in lists.items():
                    self.at[name] = len(row)
                    row += values
                self.table.append(row)
        self.n_rows = n_rows

    def row(self):
        index = lax.axis_index("vocab") * self.n_rows + lax.axis_index("rows")
        table = jnp.array(self.table, jnp.int32)
        return lax.dynamic_slice(table, (index, 0), (1, table.shape[1]))[0]


def pooled(x, groups):
    length = x.shape[0] // groups
    u = 1.0 + x
    inverse = 1.0 / u
    act = jnp.log(u) + (x - (u - 1.0)) * inverse
    square = act * act
    total = jnp.sum((square * square).reshape(groups, length, -1), axis=1)
    return total, square * act * inverse


def forward_kernel(spec, plan_ref, *refs):
    at, count, codes, n_pieces, depth, tile, final, groups, pass_rows, kept = spec
    refs = list(refs)
    sources = [(code, refs.pop(0)) for code in codes]
    pieces = [refs.pop(0) for _ in range(n_pieces)]
    if final:
        start_ref, mask_ref = refs.pop(0), refs.pop(0)
        del refs[:kept]
        slope_ref, total_ref, sparse_ref = [refs.pop(0) for _ in range(3)]
    else:
        out_ref = refs.pop(0)
    held, weights, held_sem, weight_sem = refs
    step = pl.program_id(0)

    def weight_copy(j, t, which, slot):
        return pltpu.make_async_copy(
            pieces[which].at[:, pl.ds(pl.multiple_of(j * tile, tile), tile)],
            weights.at[slot, pl.ds(t * depth, depth)],
            weight_sem.at[slot, t],
        )

    def fetch(j, slot, t):
        for which in range(n_pieces):
            pl.when(plan_ref[at + t] == which)(weight_copy(j, t, which, slot).start)

    def hidden_copy(t, ref):
        return pltpu.make_async_copy(
            ref.at[:, pl.ds(pl.multiple_of(plan_ref[at + 2 * count + t], 128), depth)],
            held.at[:, pl.ds(t * depth, depth)],
            held_sem.at[t],
        )

    @pl.when(step == 0)
    def _():
        for t in range(count):
            for code, ref in sources:
                pl.when(plan_ref[at + count + t] == code)(hidden_copy(t, ref).start)
            fetch(0, 0, t)

    slot = lax.rem(step, 2)

    @pl.when(step + 1 < pl.num_programs(0))
    def _():
        for t in range(count):
            fetch(step + 1, 1 - slot, t)

    value = None
    for t in range(count):
        block = pl.ds(t * depth, depth)

        @pl.when(step == 0)
        def _():
            hidden_copy(t, sources[0][1]).wait()

        weight_copy(step, t, 0, slot).wait()
        term = jnp.dot(held[:, block], weights[slot, block], preferred_element_type=jnp.float32)
        value = term if value is None else value + term
    if not final:
        out_ref[...] = value
        return
    mask = mask_ref[...]
    mask = jnp.concatenate([mask] * (tile // mask.shape[1]), axis=1)
    x = jnp.maximum(value + start_ref[...], 0.0) * mask
    totals = []
    for lower, upper in ((0, pass_rows), (pass_rows, x.shape[0])):
        total, slope = pooled(x[lower:upper], groups)
        slope_ref[lower:upper, :] = slope.astype(slope_ref.dtype)
        totals.append(total)
    total = jnp.concatenate(totals, axis=0)
    total_ref[...] = total
    sparse_ref[...] = (jnp.sqrt(jnp.sqrt(total + 1.0)) - 1.0).astype(sparse_ref.dtype)


def forward(found, pieces, plan, at, count, tile=512, pool=None):
    rows = found[0].shape[0]
    depth, width = pieces[0].shape
    keys = sorted(found)
    anywhere = pl.BlockSpec(memory_space=pl.ANY)
    operands = [found[key] for key in keys] + list(pieces)
    in_specs = [anywhere] * len(operands)
    groups = pass_rows = 0
    filled = ()
    if pool is not None:
        start, mask, groups, pass_rows, whole, first, filled = pool
        skip = first // tile
        column = lambda height: pl.BlockSpec((height, tile), lambda j, *_: (0, j + skip))
        operands += [start, mask]
        in_specs.append(pl.BlockSpec((rows, tile), lambda j, *_: (0, j)))
        in_specs.append(pl.BlockSpec(mask.shape, lambda j, *_: (0, 0)))
        in_specs += [anywhere] * len(filled)
        out_shape = [
            jax.ShapeDtypeStruct((rows, whole), jnp.bfloat16),
            jax.ShapeDtypeStruct((2 * groups, whole), jnp.float32),
            jax.ShapeDtypeStruct((2 * groups, whole), jnp.bfloat16),
        ]
        out_specs = [column(rows), column(2 * groups), column(2 * groups)]
    else:
        out_shape = jax.ShapeDtypeStruct((rows, width), jnp.float32)
        out_specs = pl.BlockSpec((rows, tile), lambda j, *_: (0, j))
    spec = (at, count, tuple(keys), len(pieces), depth, tile, pool is not None, groups, pass_rows, len(filled))
    return pl.pallas_call(
        functools.partial(forward_kernel, spec),
        out_shape=out_shape,
        grid_spec=pltpu.PrefetchScalarGridSpec(
            num_scalar_prefetch=1,
            grid=(width // tile,),
            in_specs=in_specs,
            out_specs=out_specs,
            scratch_shapes=[
                pltpu.VMEM((rows, count * depth), jnp.bfloat16),
                pltpu.VMEM((2, count * depth, tile), jnp.bfloat16),
                pltpu.SemaphoreType.DMA((count,)),
                pltpu.SemaphoreType.DMA((2, count)),
            ],
        ),
        input_output_aliases={1 + len(operands) + i: i for i in range(len(filled))},
        compiler_params=pltpu.CompilerParams(
            dimension_semantics=("arbitrary",), vmem_limit_bytes=VMEM_BYTES
        ),
        cost_estimate=pl.CostEstimate(
            flops=2 * rows * depth * count * width,
            bytes_accessed=count * depth * width * 2 + rows * width * 8,
            transcendentals=rows * width if pool is not None else 0,
        ),
        name="forward_part" if pool is None else "forward_final",
    )(plan, *operands, *filled)


def spans(parts):
    found, lower = [], 0
    for part in parts:
        found.append((lower, part[0].shape[1]))
        lower += part[0].shape[1]
    return found


def first_kernel(spec, plan_ref, slope_ref, pass_ref, query_ref, *refs):
    at, count, ranges, groups, pass_length, query_length, keep = spec
    parts = [refs[i * count : (i + 1) * count] for i in range(len(ranges))]
    refs = refs[count * len(ranges) :]
    (grad_ref, out_ref) = refs[:2] if keep else (refs[1], refs[0])
    held, total, sem = refs[2:]
    step = pl.program_id(0)
    tile = slope_ref.shape[1]
    steps = held.shape[0]

    def copy(j, which):
        i = [i for i, (lower, width) in enumerate(ranges) if lower <= j * tile < lower + width][0]
        return pltpu.make_async_copy(
            parts[i][which].at[:, pl.ds(j * tile - ranges[i][0], tile)], held.at[j], sem.at[j]
        )

    @pl.when(step == 0)
    def _():
        for which in range(count):

            @pl.when(plan_ref[at] == which)
            def _():
                for j in range(steps):
                    copy(j, which).start()

        total[...] = jnp.zeros_like(total)

    lower = 0
    for factor_ref, length in ((pass_ref, pass_length), (query_ref, query_length)):
        for p in range(groups):
            rows = pl.ds(lower, length)
            grad_ref[rows, :] = (slope_ref[rows, :].astype(jnp.float32) * factor_ref[p : p + 1, :]).astype(grad_ref.dtype)
            lower += length
    pltpu.make_async_copy(parts[0][0].at[:, pl.ds(0, tile)], held.at[step], sem.at[step]).wait()
    total[...] += lax.dot_general(
        grad_ref[...], held[step], (((1,), (1,)), ((), ())), preferred_element_type=jnp.float32
    )

    @pl.when(step == steps - 1)
    def _():
        out_ref[...] = total[...].astype(out_ref.dtype)


def backward_first(slopes, factor_pass, factor_query, lengths, parts, plan, at, keep, tile=1024):
    rows, width = slopes.shape
    groups = factor_pass.shape[0]
    depth = parts[0][0].shape[0]
    count = len(parts[0])
    pieces = [piece for part in parts for piece in part]
    column = lambda height: pl.BlockSpec((height, tile), lambda j, *_: (0, j))
    out_shape = [jax.ShapeDtypeStruct((rows, depth), jnp.bfloat16)]
    out_specs = [pl.BlockSpec((rows, depth), lambda j, *_: (0, 0))]
    scratch = [] if keep else [pltpu.VMEM((rows, tile), jnp.bfloat16)]
    if keep:
        out_shape.insert(0, jax.ShapeDtypeStruct((rows, width), jnp.bfloat16))
        out_specs.insert(0, column(rows))
    return pl.pallas_call(
        functools.partial(first_kernel, (at, count, spans(parts), groups) + lengths + (keep,)),
        out_shape=out_shape,
        grid_spec=pltpu.PrefetchScalarGridSpec(
            num_scalar_prefetch=1,
            grid=(width // tile,),
            in_specs=[column(rows), column(groups), column(groups)]
            + [pl.BlockSpec(memory_space=pl.ANY)] * len(pieces),
            out_specs=out_specs,
            scratch_shapes=scratch
            + [
                pltpu.VMEM((width // tile, depth, tile), jnp.bfloat16),
                pltpu.VMEM((rows, depth), jnp.float32),
                pltpu.SemaphoreType.DMA((width // tile,)),
            ],
        ),
        compiler_params=pltpu.CompilerParams(
            dimension_semantics=("arbitrary",), vmem_limit_bytes=FIRST_VMEM_BYTES
        ),
        cost_estimate=pl.CostEstimate(
            flops=2 * rows * depth * width,
            bytes_accessed=(depth * width + 2 * rows * width + rows * depth) * 2,
            transcendentals=0,
        ),
        name="backward_first",
    )(plan, slopes, factor_pass, factor_query, *pieces)


def backward_kernel(spec, plan_ref, slopes_ref, *refs):
    at_plan, count, ranges, parts, adds = spec
    units = len(adds)
    n_adds = max([0] + [i + 1 for unit in adds for i in unit])
    groups = [refs[i * count : (i + 1) * count] for i in range(len(ranges))]
    refs = refs[count * len(ranges) :]
    running, refs = refs[:n_adds], refs[n_adds:]
    outs, (held, slopes, piece_sem, slope_sem) = refs[:units], refs[units:]
    rows = slopes_ref.shape[0] // parts

    def slope_copy(i):
        at = pl.ds(pl.multiple_of(i * rows, 16), rows)
        return pltpu.make_async_copy(slopes_ref.at[at, :], slopes.at[at, :], slope_sem.at[i])

    def piece_copy(unit, i, which):
        lower, width = ranges[i]
        return pltpu.make_async_copy(
            groups[i][which], held.at[unit, :, pl.ds(lower, width)], piece_sem.at[unit, i]
        )

    for unit in range(units):
        for i in range(len(ranges)):
            for which in range(count):
                pl.when(plan_ref[at_plan + unit] == which)(piece_copy(unit, i, which).start)
        if unit == 0:
            for i in range(parts):
                slope_copy(i).start()
    for unit in range(units):
        for i in range(len(ranges)):
            piece_copy(unit, i, 0).wait()

        @pl.loop(0, parts)
        def _(i):
            if unit == 0:
                slope_copy(i).wait()
            at = pl.ds(pl.multiple_of(i * rows, 16), rows)
            value = lax.dot_general(
                slopes[at, :], held[unit], (((1,), (1,)), ((), ())), preferred_element_type=jnp.float32
            ).astype(jnp.bfloat16)
            if adds[unit]:
                value = value.astype(jnp.float32)
                for j in adds[unit]:
                    value = value + running[j][at, :].astype(jnp.float32)
            outs[unit][at, :] = value.astype(outs[unit].dtype)


def backward(slopes, groups, plan, at, running=(), adds=((),)):
    rows, width = slopes.shape
    depth = groups[0][0].shape[0]
    pieces = [piece for group in groups for piece in group]
    count, units = len(groups[0]), len(adds)
    parts = 3 if rows % 48 == 0 else 1
    whole = pl.BlockSpec(memory_space=pltpu.VMEM)
    anywhere = pl.BlockSpec(memory_space=pl.ANY)
    return pl.pallas_call(
        functools.partial(backward_kernel, (at, count, spans(groups), parts, adds)),
        out_shape=[jax.ShapeDtypeStruct((rows, depth), jnp.bfloat16)] * units,
        in_specs=[pl.BlockSpec(memory_space=pltpu.SMEM)] + [anywhere] * (1 + len(pieces)) + [whole] * len(running),
        out_specs=[whole] * units,
        scratch_shapes=[
            pltpu.VMEM((units, depth, width), jnp.bfloat16),
            pltpu.VMEM((rows, width), jnp.bfloat16),
            pltpu.SemaphoreType.DMA((units, len(groups))),
            pltpu.SemaphoreType.DMA((parts,)),
        ],
        compiler_params=pltpu.CompilerParams(vmem_limit_bytes=SMALL_VMEM_BYTES),
        cost_estimate=pl.CostEstimate(
            flops=2 * rows * depth * units * width,
            bytes_accessed=(units * depth * width + rows * width + units * rows * depth) * 2,
            transcendentals=0,
        ),
        name="backward_part",
    )(plan, slopes, *pieces, *running)


def line_reduce_scatter(first, product, n, share):
    left, right = [None] * share, [None] * share
    for step in range(1, n):
        for i in range(share):
            name = f"part{step}_{i}"
            if step == 1 and i < 2:
                to_left = to_right = first(name, i)
            elif 2 * step <= n:
                running = () if step == 1 else (left[i], right[i])
                (to_left,) = product(name, running, (tuple(range(len(running))),))
                to_right = to_left
            else:
                to_left, to_right = product(name, (left[i], right[i]), ((0,), (1,)))
            left[i] = lax.ppermute(to_left, "vocab", [(d, d - 1) for d in range(n - step, n)])
            right[i] = lax.ppermute(to_right, "vocab", [(d, d + 1) for d in range(step)])
    terms = []
    for i in range(share):
        own = product(f"own_{i}", (), ((),))[0]
        terms.append(own.astype(jnp.float32) + left[i].astype(jnp.float32) + right[i].astype(jnp.float32))
    return terms


def shards(n_vocab, n_rows, *arguments):
    return body(n_vocab, n_rows, *arguments)


def body(n_vocab, n_rows, hidden_pass, hidden_query, mask_pass, mask_query, labels, head_weight):
    groups, pass_length, part = hidden_pass.shape
    query_length = hidden_query.shape[1]
    pass_rows = groups * pass_length
    depth, width = head_weight.shape
    share = n_rows // n_vocab
    plans = Plan(n_vocab, n_rows, depth)
    plan = plans.row()
    order = plan[plans.at["order"] : plans.at["order"] + n_rows]
    tokens = jnp.concatenate(
        [hidden_pass.reshape(pass_rows, part), hidden_query.reshape(groups * query_length, part)], axis=0
    )
    mask = jnp.concatenate([mask_pass.reshape(-1), mask_query.reshape(-1)]).astype(jnp.float32)
    mask = jnp.broadcast_to(mask[:, None], (mask.shape[0], 128))
    found = line_gather(tokens, n_vocab)
    halves = 2 if two_paths(n_rows, n_vocab) and width % 2048 == 0 else 1
    part_width = width // halves
    parts = []
    for i in range(halves):
        own = head_weight
        if i > 0:
            own, _ = lax.optimization_barrier((head_weight, tokens))
        own = own[:, i * part_width : (i + 1) * part_width]
        parts.append(row_gather(own, n_rows, n_vocab))
    all_labels = jnp.stack(row_gather(labels, n_rows, n_vocab)).reshape(-1)
    passages = (order[:, None] * groups + jnp.arange(groups, dtype=jnp.int32)[None, :]).reshape(-1)
    onehot = (all_labels[:, None] == passages[None, :]).astype(jnp.float32)

    half = n_rows // 2
    near, soon = found, n_rows
    if two_paths(n_rows, n_vocab):
        near = {code: block for code, block in found.items() if abs(code) < n_vocab - 1}
        soon = n_rows - 2
    logits, filled = [], ()
    for i in range(halves):
        logits.append(forward(near, parts[i][:soon], plan, plans.at["soon"], half))
    for i in range(halves):
        pool = (logits[i], mask, groups, pass_rows, width, i * part_width, filled)
        filled = forward(found, parts[i], plan, plans.at["last"], half, pool=pool)
    slopes, totals, sparse = filled
    all_sparse = jnp.stack(row_gather(sparse, n_rows, n_vocab))
    all_pass = all_sparse[:, :groups].reshape(-1, width)
    all_query = all_sparse[:, groups:].reshape(-1, width)
    scaling = SHARPNESS * (width * n_vocab) ** (-0.5)
    scores = lax.dot_general(all_query, all_pass, (((1,), (1,)), ((), ())), preferred_element_type=jnp.float32)
    shifted = [
        lax.ppermute(scores, "vocab", [(d, (d + s) % n_vocab) for d in range(n_vocab)]) for s in range(1, n_vocab)
    ]
    for other in shifted:
        scores = scores + other
    scores = scores * scaling
    positive = jnp.sum(scores * onehot, axis=1, keepdims=True)
    weights = jax.nn.sigmoid(MARGIN + scores - positive) * (1.0 - onehot)
    score_grad = ((weights - onehot * jnp.sum(weights, axis=1, keepdims=True)) * scaling).astype(jnp.bfloat16)
    if two_paths(n_rows, n_vocab):
        of_query, of_pass = score_grad[:groups], score_grad[:, :groups]
    else:
        row = lax.axis_index("rows") * groups
        of_query = lax.dynamic_slice_in_dim(score_grad, row, groups, 0)
        of_pass = lax.dynamic_slice_in_dim(score_grad, row, groups, 1)
    query_grad = jnp.dot(of_query, all_pass, preferred_element_type=jnp.float32)
    pass_grad = lax.dot_general(of_pass, all_query, (((0,), (0,)), ((), ())), preferred_element_type=jnp.float32)
    root = jnp.sqrt(jnp.sqrt(totals + 1.0))
    cube = root * root * root
    factors = (pass_grad / cube[:groups], query_grad / cube[groups:], (pass_length, query_length))
    logit_grad = []

    def first(name, i):
        keep = i == 1 or share == 1
        *grad, block = backward_first(slopes, *factors, parts, plan, plans.at[name], keep)
        logit_grad.extend(grad)
        return block

    def product(name, running, adds):
        return backward(logit_grad[0], parts, plan, plans.at[name], running, adds)

    summed = line_reduce_scatter(first, product, n_vocab, share)
    summed = jnp.concatenate(summed, axis=1).astype(jnp.bfloat16)
    return (
        summed[:pass_rows].reshape(groups, pass_length, part),
        summed[pass_rows:].reshape(groups, query_length, part),
    )


def solution(mesh):
    n_vocab, n_rows = mesh.shape["vocab"], mesh.shape["rows"]
    return jax.shard_map(
        functools.partial(shards, n_vocab, n_rows),
        mesh=mesh,
        in_specs=(
            P("rows", None, "vocab"),
            P("rows", None, "vocab"),
            P("rows", None),
            P("rows", None),
            P("rows"),
            P("rows", "vocab"),
        ),
        out_specs=(P("rows", None, "vocab"), P("rows", None, "vocab")),
        check_vma=False,
    )
```

```python
import functools

import jax
import jax.numpy as jnp
from jax import lax
from jax.experimental import pallas as pl
from jax.experimental.pallas import tpu as pltpu
from jax.sharding import PartitionSpec as P


MARGIN = 1.0
SHARPNESS = 16.0

VMEM_BYTES = 62 * 1024 * 1024
FIRST_VMEM_BYTES = 24 * 1024 * 1024
SMALL_VMEM_BYTES = 48 * 1024 * 1024
CORES = 2


def chip_grid(n_rows):
    chips = n_rows // CORES
    tall = 1
    while (tall * 2) ** 2 <= chips and chips % (tall * 2) == 0:
        tall *= 2
    return tall, chips // tall


def line_gather(block, n):
    found = {0: block}
    left = right = block
    for step in range(1, n):
        left = lax.ppermute(left, "vocab", [(z, z - 1) for z in range(1, n - step + 1)])
        right = lax.ppermute(right, "vocab", [(z, z + 1) for z in range(step - 1, n - 1)])
        found[step] = left
        found[-step] = right
    return found


def two_paths(n_rows, n_vocab):
    return chip_grid(n_rows) == (2, 2) and n_rows == CORES * n_vocab


def row_gather(block, n_rows, n_vocab):
    if not two_paths(n_rows, n_vocab):
        whole = lax.all_gather(block, "rows", axis=0)
        return [whole[r] for r in range(n_rows)]
    x_bit, y_bit = CORES, CORES * 2
    main = [(r, r ^ (x_bit if r % CORES == 0 else y_bit)) for r in range(n_rows)]
    side = [(r, r ^ (y_bit if r % CORES == 0 else x_bit)) for r in range(n_rows)]
    twin = [(r, r ^ 1) for r in range(n_rows)]

    def move(value, pairs):
        return lax.ppermute(value, "rows", pairs)

    by_main = move(block, main)
    by_side = move(block, side)
    own_twin = move(block, twin)
    far = move(by_side, main)
    main_twin = move(by_main, twin)
    side_twin = move(by_side, twin)
    far_twin = move(far, twin)
    return [block, own_twin, by_main, side_twin, by_side, main_twin, far, far_twin]


def row_order(r, n_rows, n_vocab):
    if not two_paths(n_rows, n_vocab):
        return list(range(n_rows))
    x_bit, y_bit = CORES, CORES * 2
    along, across = (x_bit, y_bit) if r % CORES == 0 else (y_bit, x_bit)
    return [r ^ hop ^ core for hop in (0, along, across, x_bit | y_bit) for core in (0, 1)]


class Plan:
    def __init__(self, n_vocab, n_rows, depth):
        share = n_rows // n_vocab
        self.at, self.table = {}, []
        for z in range(n_vocab):
            for r in range(n_rows):
                lists = {}
                order = row_order(r, n_rows, n_vocab)
                lists["order"] = order
                half = n_rows // 2
                picks = {"soon": list(range(half)), "last": list(range(half, n_rows))}
                if two_paths(n_rows, n_vocab):
                    late = [i for i in range(3) if abs(order[2 * i] // share - z) == n_vocab - 1]
                    wait = late[0] if late else 2
                    rest = [i for i in range(4) if i != wait]
                    rest = rest[:2] + [wait, rest[2]]
                    pick = [2 * i + core for i in rest for core in range(2)]
                    picks = {"soon": pick[:half], "last": pick[half:]}
                for name, pick in picks.items():
                    lists[name] = (
                        pick
                        + [order[i] // share - z for i in pick]
                        + [order[i] % share * depth for i in pick]
                    )
                place = {row: i for i, row in enumerate(order)}
                for i in range(share):
                    of = lambda block: place[block % n_vocab * share + i]
                    for step in range(1, n_vocab):
                        if 2 * step <= n_vocab:
                            units = [z + step if z + step >= n_vocab else z - step]
                        else:
                            units = [z + step, z - step]
                        lists[f"part{step}_{i}"] = [of(block) for block in units]
                    lists[f"own_{i}"] = [of(z)]
                row = []
                for name, values in lists.items():
                    self.at[name] = len(row)
                    row += values
                self.table.append(row)
        self.n_rows = n_rows

    def row(self):
        index = lax.axis_index("vocab") * self.n_rows + lax.axis_index("rows")
        table = jnp.array(self.table, jnp.int32)
        return lax.dynamic_slice(table, (index, 0), (1, table.shape[1]))[0]


def pooled(x, groups):
    length = x.shape[0] // groups
    u = 1.0 + x
    inverse = 1.0 / u
    act = jnp.log(u) + (x - (u - 1.0)) * inverse
    square = act * act
    total = jnp.sum((square * square).reshape(groups, length, -1), axis=1)
    return total, square * act * inverse


def forward_kernel(spec, plan_ref, *refs):
    at, count, codes, n_pieces, depth, tile, final, groups, pass_rows, kept = spec
    refs = list(refs)
    sources = [(code, refs.pop(0)) for code in codes]
    pieces = [refs.pop(0) for _ in range(n_pieces)]
    if final:
        start_ref, mask_ref = refs.pop(0), refs.pop(0)
        del refs[:kept]
        slope_ref, total_ref, sparse_ref = [refs.pop(0) for _ in range(3)]
    else:
        out_ref = refs.pop(0)
    held, weights, held_sem, weight_sem = refs
    step = pl.program_id(0)

    def weight_copy(j, t, which, slot):
        return pltpu.make_async_copy(
            pieces[which].at[:, pl.ds(pl.multiple_of(j * tile, tile), tile)],
            weights.at[slot, pl.ds(t * depth, depth)],
            weight_sem.at[slot, t],
        )

    def fetch(j, slot, t):
        for which in range(n_pieces):
            pl.when(plan_ref[at + t] == which)(weight_copy(j, t, which, slot).start)

    def hidden_copy(t, ref):
        return pltpu.make_async_copy(
            ref.at[:, pl.ds(pl.multiple_of(plan_ref[at + 2 * count + t], 128), depth)],
            held.at[:, pl.ds(t * depth, depth)],
            held_sem.at[t],
        )

    @pl.when(step == 0)
    def _():
        for t in range(count):
            for code, ref in sources:
                pl.when(plan_ref[at + count + t] == code)(hidden_copy(t, ref).start)
            fetch(0, 0, t)

    slot = lax.rem(step, 2)

    @pl.when(step + 1 < pl.num_programs(0))
    def _():
        for t in range(count):
            fetch(step + 1, 1 - slot, t)

    value = None
    for t in range(count):
        block = pl.ds(t * depth, depth)

        @pl.when(step == 0)
        def _():
            hidden_copy(t, sources[0][1]).wait()

        weight_copy(step, t, 0, slot).wait()
        term = jnp.dot(held[:, block], weights[slot, block], preferred_element_type=jnp.float32)
        value = term if value is None else value + term
    if not final:
        out_ref[...] = value
        return
    mask = mask_ref[...]
    mask = jnp.concatenate([mask] * (tile // mask.shape[1]), axis=1)
    x = jnp.maximum(value + start_ref[...], 0.0) * mask
    totals = []
    for lower, upper in ((0, pass_rows), (pass_rows, x.shape[0])):
        total, slope = pooled(x[lower:upper], groups)
        slope_ref[lower:upper, :] = slope.astype(slope_ref.dtype)
        totals.append(total)
    total = jnp.concatenate(totals, axis=0)
    total_ref[...] = total
    sparse_ref[...] = (jnp.sqrt(jnp.sqrt(total + 1.0)) - 1.0).astype(sparse_ref.dtype)


def forward(found, pieces, plan, at, count, tile=512, pool=None):
    rows = found[0].shape[0]
    depth, width = pieces[0].shape
    keys = sorted(found)
    anywhere = pl.BlockSpec(memory_space=pl.ANY)
    operands = [found[key] for key in keys] + list(pieces)
    in_specs = [anywhere] * len(operands)
    groups = pass_rows = 0
    filled = ()
    if pool is not None:
        start, mask, groups, pass_rows, whole, first, filled = pool
        skip = first // tile
        column = lambda height: pl.BlockSpec((height, tile), lambda j, *_: (0, j + skip))
        operands += [start, mask]
        in_specs.append(pl.BlockSpec((rows, tile), lambda j, *_: (0, j)))
        in_specs.append(pl.BlockSpec(mask.shape, lambda j, *_: (0, 0)))
        in_specs += [anywhere] * len(filled)
        out_shape = [
            jax.ShapeDtypeStruct((rows, whole), jnp.bfloat16),
            jax.ShapeDtypeStruct((2 * groups, whole), jnp.float32),
            jax.ShapeDtypeStruct((2 * groups, width), jnp.bfloat16),
        ]
        part = pl.BlockSpec((2 * groups, tile), lambda j, *_: (0, j))
        out_specs = [column(rows), column(2 * groups), part]
    else:
        out_shape = jax.ShapeDtypeStruct((rows, width), jnp.float32)
        out_specs = pl.BlockSpec((rows, tile), lambda j, *_: (0, j))
    spec = (at, count, tuple(keys), len(pieces), depth, tile, pool is not None, groups, pass_rows, len(filled))
    return pl.pallas_call(
        functools.partial(forward_kernel, spec),
        out_shape=out_shape,
        grid_spec=pltpu.PrefetchScalarGridSpec(
            num_scalar_prefetch=1,
            grid=(width // tile,),
            in_specs=in_specs,
            out_specs=out_specs,
            scratch_shapes=[
                pltpu.VMEM((rows, count * depth), jnp.bfloat16),
                pltpu.VMEM((2, count * depth, tile), jnp.bfloat16),
                pltpu.SemaphoreType.DMA((count,)),
                pltpu.SemaphoreType.DMA((2, count)),
            ],
        ),
        input_output_aliases={1 + len(operands) + i: i for i in range(len(filled))},
        compiler_params=pltpu.CompilerParams(
            dimension_semantics=("arbitrary",), vmem_limit_bytes=VMEM_BYTES
        ),
        cost_estimate=pl.CostEstimate(
            flops=2 * rows * depth * count * width,
            bytes_accessed=count * depth * width * 2 + rows * width * 8,
            transcendentals=rows * width if pool is not None else 0,
        ),
        name="forward_part" if pool is None else "forward_final",
    )(plan, *operands, *filled)


def spans(parts):
    found, lower = [], 0
    for part in parts:
        found.append((lower, part[0].shape[1]))
        lower += part[0].shape[1]
    return found


def first_kernel(spec, plan_ref, slope_ref, pass_ref, query_ref, *refs):
    at, count, ranges, groups, pass_length, query_length, keep = spec
    parts = [refs[i * count : (i + 1) * count] for i in range(len(ranges))]
    refs = refs[count * len(ranges) :]
    (grad_ref, out_ref) = refs[:2] if keep else (refs[1], refs[0])
    held, total, sem = refs[2:]
    step = pl.program_id(0)
    tile = slope_ref.shape[1]
    steps = held.shape[0]

    def copy(j, which):
        i = [i for i, (lower, width) in enumerate(ranges) if lower <= j * tile < lower + width][0]
        return pltpu.make_async_copy(
            parts[i][which].at[:, pl.ds(j * tile - ranges[i][0], tile)], held.at[j], sem.at[j]
        )

    @pl.when(step == 0)
    def _():
        for which in range(count):

            @pl.when(plan_ref[at] == which)
            def _():
                for j in range(steps):
                    copy(j, which).start()

        total[...] = jnp.zeros_like(total)

    lower = 0
    for factor_ref, length in ((pass_ref, pass_length), (query_ref, query_length)):
        for p in range(groups):
            rows = pl.ds(lower, length)
            grad_ref[rows, :] = (slope_ref[rows, :].astype(jnp.float32) * factor_ref[p : p + 1, :]).astype(grad_ref.dtype)
            lower += length
    pltpu.make_async_copy(parts[0][0].at[:, pl.ds(0, tile)], held.at[step], sem.at[step]).wait()
    total[...] += lax.dot_general(
        grad_ref[...], held[step], (((1,), (1,)), ((), ())), preferred_element_type=jnp.float32
    )

    @pl.when(step == steps - 1)
    def _():
        out_ref[...] = total[...].astype(out_ref.dtype)


def backward_first(slopes, factor_pass, factor_query, lengths, parts, plan, at, keep, tile=1024):
    rows, width = slopes.shape
    groups = factor_pass.shape[0]
    depth = parts[0][0].shape[0]
    count = len(parts[0])
    pieces = [piece for part in parts for piece in part]
    column = lambda height: pl.BlockSpec((height, tile), lambda j, *_: (0, j))
    out_shape = [jax.ShapeDtypeStruct((rows, depth), jnp.bfloat16)]
    out_specs = [pl.BlockSpec((rows, depth), lambda j, *_: (0, 0))]
    scratch = [] if keep else [pltpu.VMEM((rows, tile), jnp.bfloat16)]
    if keep:
        out_shape.insert(0, jax.ShapeDtypeStruct((rows, width), jnp.bfloat16))
        out_specs.insert(0, column(rows))
    return pl.pallas_call(
        functools.partial(first_kernel, (at, count, spans(parts), groups) + lengths + (keep,)),
        out_shape=out_shape,
        grid_spec=pltpu.PrefetchScalarGridSpec(
            num_scalar_prefetch=1,
            grid=(width // tile,),
            in_specs=[column(rows), column(groups), column(groups)]
            + [pl.BlockSpec(memory_space=pl.ANY)] * len(pieces),
            out_specs=out_specs,
            scratch_shapes=scratch
            + [
                pltpu.VMEM((width // tile, depth, tile), jnp.bfloat16),
                pltpu.VMEM((rows, depth), jnp.float32),
                pltpu.SemaphoreType.DMA((width // tile,)),
            ],
        ),
        compiler_params=pltpu.CompilerParams(
            dimension_semantics=("arbitrary",), vmem_limit_bytes=FIRST_VMEM_BYTES
        ),
        cost_estimate=pl.CostEstimate(
            flops=2 * rows * depth * width,
            bytes_accessed=(depth * width + 2 * rows * width + rows * depth) * 2,
            transcendentals=0,
        ),
        name="backward_first",
    )(plan, slopes, factor_pass, factor_query, *pieces)


def backward_kernel(spec, plan_ref, slopes_ref, *refs):
    at_plan, count, ranges, parts, adds = spec
    units = len(adds)
    n_adds = max([0] + [i + 1 for unit in adds for i in unit])
    groups = [refs[i * count : (i + 1) * count] for i in range(len(ranges))]
    refs = refs[count * len(ranges) :]
    running, refs = refs[:n_adds], refs[n_adds:]
    outs, (held, slopes, piece_sem, slope_sem) = refs[:units], refs[units:]
    rows = slopes_ref.shape[0] // parts

    def slope_copy(i):
        at = pl.ds(pl.multiple_of(i * rows, 16), rows)
        return pltpu.make_async_copy(slopes_ref.at[at, :], slopes.at[at, :], slope_sem.at[i])

    def piece_copy(unit, i, which):
        lower, width = ranges[i]
        return pltpu.make_async_copy(
            groups[i][which], held.at[unit, :, pl.ds(lower, width)], piece_sem.at[unit, i]
        )

    for unit in range(units):
        for i in range(len(ranges)):
            for which in range(count):
                pl.when(plan_ref[at_plan + unit] == which)(piece_copy(unit, i, which).start)
        if unit == 0:
            for i in range(parts):
                slope_copy(i).start()
    for unit in range(units):
        for i in range(len(ranges)):
            piece_copy(unit, i, 0).wait()

        @pl.loop(0, parts)
        def _(i):
            if unit == 0:
                slope_copy(i).wait()
            at = pl.ds(pl.multiple_of(i * rows, 16), rows)
            value = lax.dot_general(
                slopes[at, :], held[unit], (((1,), (1,)), ((), ())), preferred_element_type=jnp.float32
            ).astype(jnp.bfloat16)
            if adds[unit]:
                value = value.astype(jnp.float32)
                for j in adds[unit]:
                    value = value + running[j][at, :].astype(jnp.float32)
            outs[unit][at, :] = value.astype(outs[unit].dtype)


def backward(slopes, groups, plan, at, running=(), adds=((),)):
    rows, width = slopes.shape
    depth = groups[0][0].shape[0]
    pieces = [piece for group in groups for piece in group]
    count, units = len(groups[0]), len(adds)
    parts = 3 if rows % 48 == 0 else 1
    whole = pl.BlockSpec(memory_space=pltpu.VMEM)
    anywhere = pl.BlockSpec(memory_space=pl.ANY)
    return pl.pallas_call(
        functools.partial(backward_kernel, (at, count, spans(groups), parts, adds)),
        out_shape=[jax.ShapeDtypeStruct((rows, depth), jnp.bfloat16)] * units,
        in_specs=[pl.BlockSpec(memory_space=pltpu.SMEM)] + [anywhere] * (1 + len(pieces)) + [whole] * len(running),
        out_specs=[whole] * units,
        scratch_shapes=[
            pltpu.VMEM((units, depth, width), jnp.bfloat16),
            pltpu.VMEM((rows, width), jnp.bfloat16),
            pltpu.SemaphoreType.DMA((units, len(groups))),
            pltpu.SemaphoreType.DMA((parts,)),
        ],
        compiler_params=pltpu.CompilerParams(vmem_limit_bytes=SMALL_VMEM_BYTES),
        cost_estimate=pl.CostEstimate(
            flops=2 * rows * depth * units * width,
            bytes_accessed=(units * depth * width + rows * width + units * rows * depth) * 2,
            transcendentals=0,
        ),
        name="backward_part",
    )(plan, slopes, *pieces, *running)


def line_reduce_scatter(first, product, n, share):
    left, right = [None] * share, [None] * share
    for step in range(1, n):
        for i in range(share):
            name = f"part{step}_{i}"
            if step == 1 and i < 2:
                to_left = to_right = first(name, i)
            elif 2 * step <= n:
                running = () if step == 1 else (left[i], right[i])
                (to_left,) = product(name, running, (tuple(range(len(running))),))
                to_right = to_left
            else:
                to_left, to_right = product(name, (left[i], right[i]), ((0,), (1,)))
            left[i] = lax.ppermute(to_left, "vocab", [(d, d - 1) for d in range(n - step, n)])
            right[i] = lax.ppermute(to_right, "vocab", [(d, d + 1) for d in range(step)])
    terms = []
    for i in range(share):
        own = product(f"own_{i}", (), ((),))[0]
        terms.append(own.astype(jnp.float32) + left[i].astype(jnp.float32) + right[i].astype(jnp.float32))
    return terms


def shards(n_vocab, n_rows, *arguments):
    return body(n_vocab, n_rows, *arguments)


def body(n_vocab, n_rows, hidden_pass, hidden_query, mask_pass, mask_query, labels, head_weight):
    groups, pass_length, part = hidden_pass.shape
    query_length = hidden_query.shape[1]
    pass_rows = groups * pass_length
    depth, width = head_weight.shape
    share = n_rows // n_vocab
    plans = Plan(n_vocab, n_rows, depth)
    plan = plans.row()
    order = plan[plans.at["order"] : plans.at["order"] + n_rows]
    tokens = jnp.concatenate(
        [hidden_pass.reshape(pass_rows, part), hidden_query.reshape(groups * query_length, part)], axis=0
    )
    mask = jnp.concatenate([mask_pass.reshape(-1), mask_query.reshape(-1)]).astype(jnp.float32)
    mask = jnp.broadcast_to(mask[:, None], (mask.shape[0], 128))
    found = line_gather(tokens, n_vocab)
    halves = 2 if two_paths(n_rows, n_vocab) and width % 2048 == 0 else 1
    part_width = width // halves
    parts = []
    for i in range(halves):
        own = head_weight
        if i > 0:
            own, _ = lax.optimization_barrier((head_weight, tokens))
        own = own[:, i * part_width : (i + 1) * part_width]
        parts.append(row_gather(own, n_rows, n_vocab))
    all_labels = jnp.stack(row_gather(labels, n_rows, n_vocab)).reshape(-1)
    passages = (order[:, None] * groups + jnp.arange(groups, dtype=jnp.int32)[None, :]).reshape(-1)
    onehot = (all_labels[:, None] == passages[None, :]).astype(jnp.float32)

    half = n_rows // 2
    near, soon = found, n_rows
    if two_paths(n_rows, n_vocab):
        near = {code: block for code, block in found.items() if abs(code) < n_vocab - 1}
        soon = n_rows - 2
    logits, filled, gathered = [], (), []
    for i in range(halves):
        logits.append(forward(near, parts[i][:soon], plan, plans.at["soon"], half))
    for i in range(halves):
        pool = (logits[i], mask, groups, pass_rows, width, i * part_width, filled)
        *filled, sparse = forward(found, parts[i], plan, plans.at["last"], half, pool=pool)
        gathered.append(jnp.stack(row_gather(sparse, n_rows, n_vocab)))
    slopes, totals = filled
    all_pass = [block[:, :groups].reshape(-1, part_width) for block in gathered]
    all_query = [block[:, groups:].reshape(-1, part_width) for block in gathered]
    scaling = SHARPNESS * (width * n_vocab) ** (-0.5)
    scores = sum(
        lax.dot_general(q, p, (((1,), (1,)), ((), ())), preferred_element_type=jnp.float32)
        for q, p in zip(all_query, all_pass)
    )
    shifted = [
        lax.ppermute(scores, "vocab", [(d, (d + s) % n_vocab) for d in range(n_vocab)]) for s in range(1, n_vocab)
    ]
    for other in shifted:
        scores = scores + other
    scores = scores * scaling
    positive = jnp.sum(scores * onehot, axis=1, keepdims=True)
    weights = jax.nn.sigmoid(MARGIN + scores - positive) * (1.0 - onehot)
    score_grad = ((weights - onehot * jnp.sum(weights, axis=1, keepdims=True)) * scaling).astype(jnp.bfloat16)
    if two_paths(n_rows, n_vocab):
        of_query, of_pass = score_grad[:groups], score_grad[:, :groups]
    else:
        row = lax.axis_index("rows") * groups
        of_query = lax.dynamic_slice_in_dim(score_grad, row, groups, 0)
        of_pass = lax.dynamic_slice_in_dim(score_grad, row, groups, 1)
    query_grad = jnp.concatenate(
        [jnp.dot(of_query, p, preferred_element_type=jnp.float32) for p in all_pass], axis=1
    )
    pass_grad = jnp.concatenate(
        [
            lax.dot_general(of_pass, q, (((0,), (0,)), ((), ())), preferred_element_type=jnp.float32)
            for q in all_query
        ],
        axis=1,
    )
    root = jnp.sqrt(jnp.sqrt(totals + 1.0))
    cube = root * root * root
    factors = (pass_grad / cube[:groups], query_grad / cube[groups:], (pass_length, query_length))
    logit_grad = []

    def first(name, i):
        keep = i == 1 or share == 1
        *grad, block = backward_first(slopes, *factors, parts, plan, plans.at[name], keep)
        logit_grad.extend(grad)
        return block

    def product(name, running, adds):
        return backward(logit_grad[0], parts, plan, plans.at[name], running, adds)

    summed = line_reduce_scatter(first, product, n_vocab, share)
    summed = jnp.concatenate(summed, axis=1).astype(jnp.bfloat16)
    return (
        summed[:pass_rows].reshape(groups, pass_length, part),
        summed[pass_rows:].reshape(groups, query_length, part),
    )


def solution(mesh):
    n_vocab, n_rows = mesh.shape["vocab"], mesh.shape["rows"]
    return jax.shard_map(
        functools.partial(shards, n_vocab, n_rows),
        mesh=mesh,
        in_specs=(
            P("rows", None, "vocab"),
            P("rows", None, "vocab"),
            P("rows", None),
            P("rows", None),
            P("rows"),
            P("rows", "vocab"),
        ),
        out_specs=(P("rows", None, "vocab"), P("rows", None, "vocab")),
        check_vma=False,
    )
```

```python
import functools

import jax
import jax.numpy as jnp
from jax import lax
from jax.experimental import pallas as pl
from jax.experimental.pallas import tpu as pltpu
from jax.sharding import PartitionSpec as P


MARGIN = 1.0
SHARPNESS = 16.0

VMEM_BYTES = 62 * 1024 * 1024
FIRST_VMEM_BYTES = 24 * 1024 * 1024
SMALL_VMEM_BYTES = 48 * 1024 * 1024
CORES = 2


def chip_grid(n_rows):
    chips = n_rows // CORES
    tall = 1
    while (tall * 2) ** 2 <= chips and chips % (tall * 2) == 0:
        tall *= 2
    return tall, chips // tall


def line_gather(block, n):
    found = {0: block}
    left = right = block
    for step in range(1, n):
        left = lax.ppermute(left, "vocab", [(z, z - 1) for z in range(1, n - step + 1)])
        right = lax.ppermute(right, "vocab", [(z, z + 1) for z in range(step - 1, n - 1)])
        found[step] = left
        found[-step] = right
    return found


def two_paths(n_rows, n_vocab):
    return chip_grid(n_rows) == (2, 2) and n_rows == CORES * n_vocab


def row_gather(block, n_rows, n_vocab, late=False):
    if not two_paths(n_rows, n_vocab):
        whole = lax.all_gather(block, "rows", axis=0)
        return [whole[r] for r in range(n_rows)]
    x_bit, y_bit = CORES, CORES * 2
    main = [(r, r ^ (x_bit if r % CORES == 0 else y_bit)) for r in range(n_rows)]
    side = [(r, r ^ (y_bit if r % CORES == 0 else x_bit)) for r in range(n_rows)]
    twin = [(r, r ^ 1) for r in range(n_rows)]

    def move(value, pairs):
        return lax.ppermute(value, "rows", pairs)

    by_main = move(block, main)
    by_side = move(block, side)
    own_twin = move(block, twin)
    far = move(by_side, main)
    main_twin = move(by_main, twin)
    side_twin = move(by_side, twin)
    far_twin = move(far, twin)
    if late:
        block, side_twin = lax.optimization_barrier((block, side_twin))
    return [block, own_twin, by_main, side_twin, by_side, main_twin, far, far_twin]


def row_order(r, n_rows, n_vocab):
    if not two_paths(n_rows, n_vocab):
        return list(range(n_rows))
    x_bit, y_bit = CORES, CORES * 2
    along, across = (x_bit, y_bit) if r % CORES == 0 else (y_bit, x_bit)
    return [r ^ hop ^ core for hop in (0, along, across, x_bit | y_bit) for core in (0, 1)]


class Plan:
    def __init__(self, n_vocab, n_rows, depth):
        share = n_rows // n_vocab
        self.at, self.table = {}, []
        for z in range(n_vocab):
            for r in range(n_rows):
                lists = {}
                order = row_order(r, n_rows, n_vocab)
                lists["order"] = order
                half = n_rows // 2
                picks = {"soon": list(range(half)), "last": list(range(half, n_rows))}
                if two_paths(n_rows, n_vocab):
                    late = [i for i in range(3) if abs(order[2 * i] // share - z) == n_vocab - 1]
                    wait = late[0] if late else 2
                    rest = [i for i in range(4) if i != wait]
                    rest = rest[:2] + [wait, rest[2]]
                    pick = [2 * i + core for i in rest for core in range(2)]
                    picks = {"soon": pick[:half], "last": pick[half:]}
                for name, pick in picks.items():
                    lists[name] = (
                        pick
                        + [order[i] // share - z for i in pick]
                        + [order[i] % share * depth for i in pick]
                    )
                place = {row: i for i, row in enumerate(order)}
                for i in range(share):
                    of = lambda block: place[block % n_vocab * share + i]
                    for step in range(1, n_vocab):
                        if 2 * step <= n_vocab:
                            units = [z + step if z + step >= n_vocab else z - step]
                        else:
                            units = [z + step, z - step]
                        lists[f"part{step}_{i}"] = [of(block) for block in units]
                    lists[f"own_{i}"] = [of(z)]
                row = []
                for name, values in lists.items():
                    self.at[name] = len(row)
                    row += values
                self.table.append(row)
        self.n_rows = n_rows

    def row(self):
        index = lax.axis_index("vocab") * self.n_rows + lax.axis_index("rows")
        table = jnp.array(self.table, jnp.int32)
        return lax.dynamic_slice(table, (index, 0), (1, table.shape[1]))[0]


def pooled(x, groups):
    length = x.shape[0] // groups
    u = 1.0 + x
    inverse = 1.0 / u
    act = jnp.log(u) + (x - (u - 1.0)) * inverse
    square = act * act
    total = jnp.sum((square * square).reshape(groups, length, -1), axis=1)
    return total, square * act * inverse


def forward_kernel(spec, plan_ref, *refs):
    at, count, codes, n_pieces, depth, tile, final, groups, pass_rows, kept = spec
    refs = list(refs)
    sources = [(code, refs.pop(0)) for code in codes]
    pieces = [refs.pop(0) for _ in range(n_pieces)]
    if final:
        start_ref, mask_ref = refs.pop(0), refs.pop(0)
        del refs[:kept]
        slope_ref, total_ref, sparse_ref = [refs.pop(0) for _ in range(3)]
    else:
        out_ref = refs.pop(0)
    held, weights, held_sem, weight_sem = refs
    step = pl.program_id(0)

    def weight_copy(j, t, which, slot):
        return pltpu.make_async_copy(
            pieces[which].at[:, pl.ds(pl.multiple_of(j * tile, tile), tile)],
            weights.at[slot, pl.ds(t * depth, depth)],
            weight_sem.at[slot, t],
        )

    def fetch(j, slot, t):
        for which in range(n_pieces):
            pl.when(plan_ref[at + t] == which)(weight_copy(j, t, which, slot).start)

    def hidden_copy(t, ref):
        return pltpu.make_async_copy(
            ref.at[:, pl.ds(pl.multiple_of(plan_ref[at + 2 * count + t], 128), depth)],
            held.at[:, pl.ds(t * depth, depth)],
            held_sem.at[t],
        )

    @pl.when(step == 0)
    def _():
        for t in range(count):
            for code, ref in sources:
                pl.when(plan_ref[at + count + t] == code)(hidden_copy(t, ref).start)
            fetch(0, 0, t)

    slot = lax.rem(step, 2)

    @pl.when(step + 1 < pl.num_programs(0))
    def _():
        for t in range(count):
            fetch(step + 1, 1 - slot, t)

    value = None
    for t in range(count):
        block = pl.ds(t * depth, depth)

        @pl.when(step == 0)
        def _():
            hidden_copy(t, sources[0][1]).wait()

        weight_copy(step, t, 0, slot).wait()
        term = jnp.dot(held[:, block], weights[slot, block], preferred_element_type=jnp.float32)
        value = term if value is None else value + term
    if not final:
        out_ref[...] = value
        return
    mask = mask_ref[...]
    mask = jnp.concatenate([mask] * (tile // mask.shape[1]), axis=1)
    x = jnp.maximum(value + start_ref[...], 0.0) * mask
    totals = []
    for lower, upper in ((0, pass_rows), (pass_rows, x.shape[0])):
        total, slope = pooled(x[lower:upper], groups)
        slope_ref[lower:upper, :] = slope.astype(slope_ref.dtype)
        totals.append(total)
    total = jnp.concatenate(totals, axis=0)
    total_ref[...] = total
    sparse_ref[...] = (jnp.sqrt(jnp.sqrt(total + 1.0)) - 1.0).astype(sparse_ref.dtype)


def forward(found, pieces, plan, at, count, tile=512, pool=None):
    rows = found[0].shape[0]
    depth, width = pieces[0].shape
    keys = sorted(found)
    anywhere = pl.BlockSpec(memory_space=pl.ANY)
    operands = [found[key] for key in keys] + list(pieces)
    in_specs = [anywhere] * len(operands)
    groups = pass_rows = 0
    filled = ()
    if pool is not None:
        start, mask, groups, pass_rows, whole, first, filled = pool
        skip = first // tile
        column = lambda height: pl.BlockSpec((height, tile), lambda j, *_: (0, j + skip))
        operands += [start, mask]
        in_specs.append(pl.BlockSpec((rows, tile), lambda j, *_: (0, j)))
        in_specs.append(pl.BlockSpec(mask.shape, lambda j, *_: (0, 0)))
        in_specs += [anywhere] * len(filled)
        out_shape = [
            jax.ShapeDtypeStruct((rows, whole), jnp.bfloat16),
            jax.ShapeDtypeStruct((2 * groups, whole), jnp.float32),
            jax.ShapeDtypeStruct((2 * groups, width), jnp.bfloat16),
        ]
        part = pl.BlockSpec((2 * groups, tile), lambda j, *_: (0, j))
        out_specs = [column(rows), column(2 * groups), part]
    else:
        out_shape = jax.ShapeDtypeStruct((rows, width), jnp.float32)
        out_specs = pl.BlockSpec((rows, tile), lambda j, *_: (0, j))
    spec = (at, count, tuple(keys), len(pieces), depth, tile, pool is not None, groups, pass_rows, len(filled))
    return pl.pallas_call(
        functools.partial(forward_kernel, spec),
        out_shape=out_shape,
        grid_spec=pltpu.PrefetchScalarGridSpec(
            num_scalar_prefetch=1,
            grid=(width // tile,),
            in_specs=in_specs,
            out_specs=out_specs,
            scratch_shapes=[
                pltpu.VMEM((rows, count * depth), jnp.bfloat16),
                pltpu.VMEM((2, count * depth, tile), jnp.bfloat16),
                pltpu.SemaphoreType.DMA((count,)),
                pltpu.SemaphoreType.DMA((2, count)),
            ],
        ),
        input_output_aliases={1 + len(operands) + i: i for i in range(len(filled))},
        compiler_params=pltpu.CompilerParams(
            dimension_semantics=("arbitrary",), vmem_limit_bytes=VMEM_BYTES
        ),
        cost_estimate=pl.CostEstimate(
            flops=2 * rows * depth * count * width,
            bytes_accessed=count * depth * width * 2 + rows * width * 8,
            transcendentals=rows * width if pool is not None else 0,
        ),
        name="forward_part" if pool is None else "forward_final",
    )(plan, *operands, *filled)


def spans(parts):
    found, lower = [], 0
    for part in parts:
        found.append((lower, part[0].shape[1]))
        lower += part[0].shape[1]
    return found


def first_kernel(spec, plan_ref, slope_ref, pass_ref, query_ref, *refs):
    at, count, ranges, groups, pass_length, query_length, keep = spec
    parts = [refs[i * count : (i + 1) * count] for i in range(len(ranges))]
    refs = refs[count * len(ranges) :]
    (grad_ref, out_ref) = refs[:2] if keep else (refs[1], refs[0])
    held, total, sem = refs[2:]
    step = pl.program_id(0)
    tile = slope_ref.shape[1]
    steps = held.shape[0]

    def copy(j, which):
        i = [i for i, (lower, width) in enumerate(ranges) if lower <= j * tile < lower + width][0]
        return pltpu.make_async_copy(
            parts[i][which].at[:, pl.ds(j * tile - ranges[i][0], tile)], held.at[j], sem.at[j]
        )

    @pl.when(step == 0)
    def _():
        for which in range(count):

            @pl.when(plan_ref[at] == which)
            def _():
                for j in range(steps):
                    copy(j, which).start()

        total[...] = jnp.zeros_like(total)

    lower = 0
    for factor_ref, length in ((pass_ref, pass_length), (query_ref, query_length)):
        for p in range(groups):
            rows = pl.ds(lower, length)
            grad_ref[rows, :] = (slope_ref[rows, :].astype(jnp.float32) * factor_ref[p : p + 1, :]).astype(grad_ref.dtype)
            lower += length
    pltpu.make_async_copy(parts[0][0].at[:, pl.ds(0, tile)], held.at[step], sem.at[step]).wait()
    total[...] += lax.dot_general(
        grad_ref[...], held[step], (((1,), (1,)), ((), ())), preferred_element_type=jnp.float32
    )

    @pl.when(step == steps - 1)
    def _():
        out_ref[...] = total[...].astype(out_ref.dtype)


def backward_first(slopes, factor_pass, factor_query, lengths, parts, plan, at, keep, tile=1024):
    rows, width = slopes.shape
    groups = factor_pass.shape[0]
    depth = parts[0][0].shape[0]
    count = len(parts[0])
    pieces = [piece for part in parts for piece in part]
    column = lambda height: pl.BlockSpec((height, tile), lambda j, *_: (0, j))
    out_shape = [jax.ShapeDtypeStruct((rows, depth), jnp.bfloat16)]
    out_specs = [pl.BlockSpec((rows, depth), lambda j, *_: (0, 0))]
    scratch = [] if keep else [pltpu.VMEM((rows, tile), jnp.bfloat16)]
    if keep:
        out_shape.insert(0, jax.ShapeDtypeStruct((rows, width), jnp.bfloat16))
        out_specs.insert(0, column(rows))
    return pl.pallas_call(
        functools.partial(first_kernel, (at, count, spans(parts), groups) + lengths + (keep,)),
        out_shape=out_shape,
        grid_spec=pltpu.PrefetchScalarGridSpec(
            num_scalar_prefetch=1,
            grid=(width // tile,),
            in_specs=[column(rows), column(groups), column(groups)]
            + [pl.BlockSpec(memory_space=pl.ANY)] * len(pieces),
            out_specs=out_specs,
            scratch_shapes=scratch
            + [
                pltpu.VMEM((width // tile, depth, tile), jnp.bfloat16),
                pltpu.VMEM((rows, depth), jnp.float32),
                pltpu.SemaphoreType.DMA((width // tile,)),
            ],
        ),
        compiler_params=pltpu.CompilerParams(
            dimension_semantics=("arbitrary",), vmem_limit_bytes=FIRST_VMEM_BYTES
        ),
        cost_estimate=pl.CostEstimate(
            flops=2 * rows * depth * width,
            bytes_accessed=(depth * width + 2 * rows * width + rows * depth) * 2,
            transcendentals=0,
        ),
        name="backward_first",
    )(plan, slopes, factor_pass, factor_query, *pieces)


def backward_kernel(spec, plan_ref, slopes_ref, *refs):
    at_plan, count, ranges, parts, adds = spec
    units = len(adds)
    n_adds = max([0] + [i + 1 for unit in adds for i in unit])
    groups = [refs[i * count : (i + 1) * count] for i in range(len(ranges))]
    refs = refs[count * len(ranges) :]
    running, refs = refs[:n_adds], refs[n_adds:]
    outs, (held, slopes, piece_sem, slope_sem) = refs[:units], refs[units:]
    rows = slopes_ref.shape[0] // parts

    def slope_copy(i):
        at = pl.ds(pl.multiple_of(i * rows, 16), rows)
        return pltpu.make_async_copy(slopes_ref.at[at, :], slopes.at[at, :], slope_sem.at[i])

    def piece_copy(unit, i, which):
        lower, width = ranges[i]
        return pltpu.make_async_copy(
            groups[i][which], held.at[unit, :, pl.ds(lower, width)], piece_sem.at[unit, i]
        )

    for unit in range(units):
        for i in range(len(ranges)):
            for which in range(count):
                pl.when(plan_ref[at_plan + unit] == which)(piece_copy(unit, i, which).start)
        if unit == 0:
            for i in range(parts):
                slope_copy(i).start()
    for unit in range(units):
        for i in range(len(ranges)):
            piece_copy(unit, i, 0).wait()

        @pl.loop(0, parts)
        def _(i):
            if unit == 0:
                slope_copy(i).wait()
            at = pl.ds(pl.multiple_of(i * rows, 16), rows)
            value = lax.dot_general(
                slopes[at, :], held[unit], (((1,), (1,)), ((), ())), preferred_element_type=jnp.float32
            ).astype(jnp.bfloat16)
            if adds[unit]:
                value = value.astype(jnp.float32)
                for j in adds[unit]:
                    value = value + running[j][at, :].astype(jnp.float32)
            outs[unit][at, :] = value.astype(outs[unit].dtype)


def backward(slopes, groups, plan, at, running=(), adds=((),)):
    rows, width = slopes.shape
    depth = groups[0][0].shape[0]
    pieces = [piece for group in groups for piece in group]
    count, units = len(groups[0]), len(adds)
    parts = 3 if rows % 48 == 0 else 1
    whole = pl.BlockSpec(memory_space=pltpu.VMEM)
    anywhere = pl.BlockSpec(memory_space=pl.ANY)
    return pl.pallas_call(
        functools.partial(backward_kernel, (at, count, spans(groups), parts, adds)),
        out_shape=[jax.ShapeDtypeStruct((rows, depth), jnp.bfloat16)] * units,
        in_specs=[pl.BlockSpec(memory_space=pltpu.SMEM)] + [anywhere] * (1 + len(pieces)) + [whole] * len(running),
        out_specs=[whole] * units,
        scratch_shapes=[
            pltpu.VMEM((units, depth, width), jnp.bfloat16),
            pltpu.VMEM((rows, width), jnp.bfloat16),
            pltpu.SemaphoreType.DMA((units, len(groups))),
            pltpu.SemaphoreType.DMA((parts,)),
        ],
        compiler_params=pltpu.CompilerParams(vmem_limit_bytes=SMALL_VMEM_BYTES),
        cost_estimate=pl.CostEstimate(
            flops=2 * rows * depth * units * width,
            bytes_accessed=(units * depth * width + rows * width + units * rows * depth) * 2,
            transcendentals=0,
        ),
        name="backward_part",
    )(plan, slopes, *pieces, *running)


def line_reduce_scatter(first, product, n, share):
    left, right = [None] * share, [None] * share
    for step in range(1, n):
        for i in range(share):
            name = f"part{step}_{i}"
            if step == 1 and i < 2:
                to_left = to_right = first(name, i)
            elif 2 * step <= n:
                running = () if step == 1 else (left[i], right[i])
                (to_left,) = product(name, running, (tuple(range(len(running))),))
                to_right = to_left
            else:
                to_left, to_right = product(name, (left[i], right[i]), ((0,), (1,)))
            left[i] = lax.ppermute(to_left, "vocab", [(d, d - 1) for d in range(n - step, n)])
            right[i] = lax.ppermute(to_right, "vocab", [(d, d + 1) for d in range(step)])
    terms = []
    for i in range(share):
        early = i + 1 < share
        running = (left[i], right[i]) if early else ()
        own = product(f"own_{i}", running, (tuple(range(len(running))),))[0]
        if not early:
            own = own.astype(jnp.float32) + left[i].astype(jnp.float32) + right[i].astype(jnp.float32)
        terms.append(own.astype(jnp.bfloat16))
    return terms


def shards(n_vocab, n_rows, *arguments):
    return body(n_vocab, n_rows, *arguments)


def body(n_vocab, n_rows, hidden_pass, hidden_query, mask_pass, mask_query, labels, head_weight):
    groups, pass_length, part = hidden_pass.shape
    query_length = hidden_query.shape[1]
    pass_rows = groups * pass_length
    depth, width = head_weight.shape
    share = n_rows // n_vocab
    plans = Plan(n_vocab, n_rows, depth)
    plan = plans.row()
    order = plan[plans.at["order"] : plans.at["order"] + n_rows]
    tokens = jnp.concatenate(
        [hidden_pass.reshape(pass_rows, part), hidden_query.reshape(groups * query_length, part)], axis=0
    )
    mask = jnp.concatenate([mask_pass.reshape(-1), mask_query.reshape(-1)]).astype(jnp.float32)
    mask = jnp.broadcast_to(mask[:, None], (mask.shape[0], 128))
    found = line_gather(tokens, n_vocab)
    halves = 2 if two_paths(n_rows, n_vocab) and width % 2048 == 0 else 1
    part_width = width // halves
    parts = []
    for i in range(halves):
        own = head_weight
        if i > 0:
            own, _ = lax.optimization_barrier((head_weight, tokens))
        own = own[:, i * part_width : (i + 1) * part_width]
        parts.append(row_gather(own, n_rows, n_vocab))
    all_labels = jnp.stack(row_gather(labels, n_rows, n_vocab)).reshape(-1)
    passages = (order[:, None] * groups + jnp.arange(groups, dtype=jnp.int32)[None, :]).reshape(-1)
    onehot = (all_labels[:, None] == passages[None, :]).astype(jnp.float32)

    half = n_rows // 2
    near, soon = found, n_rows
    if two_paths(n_rows, n_vocab):
        near = {code: block for code, block in found.items() if abs(code) < n_vocab - 1}
        soon = n_rows - 2
    logits, filled, gathered = [], (), []
    for i in range(halves):
        logits.append(forward(near, parts[i][:soon], plan, plans.at["soon"], half))
    for i in range(halves):
        pool = (logits[i], mask, groups, pass_rows, width, i * part_width, filled)
        *filled, sparse = forward(found, parts[i], plan, plans.at["last"], half, pool=pool)
        gathered.append(jnp.stack(row_gather(sparse, n_rows, n_vocab, late=True)))
    slopes, totals = filled
    all_pass = [block[:, :groups].reshape(-1, part_width) for block in gathered]
    all_query = [block[:, groups:].reshape(-1, part_width) for block in gathered]
    scaling = SHARPNESS * (width * n_vocab) ** (-0.5)
    scores = sum(
        lax.dot_general(q, p, (((1,), (1,)), ((), ())), preferred_element_type=jnp.float32)
        for q, p in zip(all_query, all_pass)
    )
    shifted = [
        lax.ppermute(scores, "vocab", [(d, (d + s) % n_vocab) for d in range(n_vocab)]) for s in range(1, n_vocab)
    ]
    for other in shifted:
        scores = scores + other
    scores = scores * scaling
    positive = jnp.sum(scores * onehot, axis=1, keepdims=True)
    weights = jax.nn.sigmoid(MARGIN + scores - positive) * (1.0 - onehot)
    score_grad = ((weights - onehot * jnp.sum(weights, axis=1, keepdims=True)) * scaling).astype(jnp.bfloat16)
    if two_paths(n_rows, n_vocab):
        of_query, of_pass = score_grad[:groups], score_grad[:, :groups]
    else:
        row = lax.axis_index("rows") * groups
        of_query = lax.dynamic_slice_in_dim(score_grad, row, groups, 0)
        of_pass = lax.dynamic_slice_in_dim(score_grad, row, groups, 1)
    query_grad = jnp.concatenate(
        [jnp.dot(of_query, p, preferred_element_type=jnp.float32) for p in all_pass], axis=1
    )
    pass_grad = jnp.concatenate(
        [
            lax.dot_general(of_pass, q, (((0,), (0,)), ((), ())), preferred_element_type=jnp.float32)
            for q in all_query
        ],
        axis=1,
    )
    root = jnp.sqrt(jnp.sqrt(totals + 1.0))
    cube = root * root * root
    factors = (pass_grad / cube[:groups], query_grad / cube[groups:], (pass_length, query_length))
    logit_grad = []

    def first(name, i):
        keep = i == 1 or share == 1
        *grad, block = backward_first(slopes, *factors, parts, plan, plans.at[name], keep)
        logit_grad.extend(grad)
        return block

    def product(name, running, adds):
        return backward(logit_grad[0], parts, plan, plans.at[name], running, adds)

    summed = line_reduce_scatter(first, product, n_vocab, share)
    summed = jnp.concatenate(summed, axis=1)
    return (
        summed[:pass_rows].reshape(groups, pass_length, part),
        summed[pass_rows:].reshape(groups, query_length, part),
    )


def solution(mesh):
    n_vocab, n_rows = mesh.shape["vocab"], mesh.shape["rows"]
    return jax.shard_map(
        functools.partial(shards, n_vocab, n_rows),
        mesh=mesh,
        in_specs=(
            P("rows", None, "vocab"),
            P("rows", None, "vocab"),
            P("rows", None),
            P("rows", None),
            P("rows"),
            P("rows", "vocab"),
        ),
        out_specs=(P("rows", None, "vocab"), P("rows", None, "vocab")),
        check_vma=False,
    )
```

```python
import functools

import jax
import jax.numpy as jnp
from jax import lax
from jax.experimental import pallas as pl
from jax.experimental.pallas import tpu as pltpu
from jax.sharding import PartitionSpec as P


MARGIN = 1.0
SHARPNESS = 16.0

VMEM_BYTES = 62 * 1024 * 1024
FIRST_VMEM_BYTES = 24 * 1024 * 1024
SMALL_VMEM_BYTES = 48 * 1024 * 1024
CORES = 2


def chip_grid(n_rows):
    chips = n_rows // CORES
    tall = 1
    while (tall * 2) ** 2 <= chips and chips % (tall * 2) == 0:
        tall *= 2
    return tall, chips // tall


def line_gather(block, n):
    found = {0: block}
    left = right = block
    for step in range(1, n):
        left = lax.ppermute(left, "vocab", [(z, z - 1) for z in range(1, n - step + 1)])
        right = lax.ppermute(right, "vocab", [(z, z + 1) for z in range(step - 1, n - 1)])
        found[step] = left
        found[-step] = right
    return found


def two_paths(n_rows, n_vocab):
    return chip_grid(n_rows) == (2, 2) and n_rows == CORES * n_vocab


def row_gather(block, n_rows, n_vocab, late=False):
    if not two_paths(n_rows, n_vocab):
        whole = lax.all_gather(block, "rows", axis=0)
        return [whole[r] for r in range(n_rows)]
    x_bit, y_bit = CORES, CORES * 2
    main = [(r, r ^ (x_bit if r % CORES == 0 else y_bit)) for r in range(n_rows)]
    side = [(r, r ^ (y_bit if r % CORES == 0 else x_bit)) for r in range(n_rows)]
    twin = [(r, r ^ 1) for r in range(n_rows)]

    def move(value, pairs):
        return lax.ppermute(value, "rows", pairs)

    by_main = move(block, main)
    by_side = move(block, side)
    own_twin = move(block, twin)
    far = move(by_side, main)
    main_twin = move(by_main, twin)
    side_twin = move(by_side, twin)
    far_twin = move(far, twin)
    if late:
        block, side_twin = lax.optimization_barrier((block, side_twin))
    return [block, own_twin, by_main, side_twin, by_side, main_twin, far, far_twin]


def row_order(r, n_rows, n_vocab):
    if not two_paths(n_rows, n_vocab):
        return list(range(n_rows))
    x_bit, y_bit = CORES, CORES * 2
    along, across = (x_bit, y_bit) if r % CORES == 0 else (y_bit, x_bit)
    return [r ^ hop ^ core for hop in (0, along, across, x_bit | y_bit) for core in (0, 1)]


class Plan:
    def __init__(self, n_vocab, n_rows, depth):
        share = n_rows // n_vocab
        self.at, self.table = {}, []
        for z in range(n_vocab):
            for r in range(n_rows):
                lists = {}
                order = row_order(r, n_rows, n_vocab)
                lists["order"] = order
                half = n_rows // 2
                picks = {"soon": list(range(half)), "last": list(range(half, n_rows))}
                if two_paths(n_rows, n_vocab):
                    late = [i for i in range(3) if abs(order[2 * i] // share - z) == n_vocab - 1]
                    wait = late[0] if late else 2
                    rest = [i for i in range(4) if i != wait]
                    rest = rest[:2] + [wait, rest[2]]
                    pick = [2 * i + core for i in rest for core in range(2)]
                    picks = {"soon": pick[:half], "last": pick[half:]}
                for name, pick in picks.items():
                    lists[name] = (
                        pick
                        + [order[i] // share - z for i in pick]
                        + [order[i] % share * depth for i in pick]
                    )
                place = {row: i for i, row in enumerate(order)}
                for i in range(share):
                    of = lambda block: place[block % n_vocab * share + i]
                    for step in range(1, n_vocab):
                        if 2 * step <= n_vocab:
                            units = [z + step if z + step >= n_vocab else z - step]
                        else:
                            units = [z + step, z - step]
                        lists[f"part{step}_{i}"] = [of(block) for block in units]
                    lists[f"own_{i}"] = [of(z)]
                row = []
                for name, values in lists.items():
                    self.at[name] = len(row)
                    row += values
                self.table.append(row)
        self.n_rows = n_rows

    def row(self):
        index = lax.axis_index("vocab") * self.n_rows + lax.axis_index("rows")
        table = jnp.array(self.table, jnp.int32)
        return lax.dynamic_slice(table, (index, 0), (1, table.shape[1]))[0]


def pooled(x, groups):
    length = x.shape[0] // groups
    u = 1.0 + x
    inverse = 1.0 / u
    act = jnp.log(u) + (x - (u - 1.0)) * inverse
    square = act * act
    total = jnp.sum((square * square).reshape(groups, length, -1), axis=1)
    return total, square * act * inverse


def forward_kernel(spec, plan_ref, *refs):
    at, count, codes, n_pieces, depth, tile, final, groups, pass_rows, kept = spec
    refs = list(refs)
    sources = [(code, refs.pop(0)) for code in codes]
    pieces = [refs.pop(0) for _ in range(n_pieces)]
    if final:
        start_ref, mask_ref = refs.pop(0), refs.pop(0)
        del refs[:kept]
        slope_ref, total_ref, sparse_ref = [refs.pop(0) for _ in range(3)]
    else:
        out_ref = refs.pop(0)
    held, weights, held_sem, weight_sem = refs
    step = pl.program_id(0)

    def weight_copy(j, t, which, slot):
        return pltpu.make_async_copy(
            pieces[which].at[:, pl.ds(pl.multiple_of(j * tile, tile), tile)],
            weights.at[slot, pl.ds(t * depth, depth)],
            weight_sem.at[slot, t],
        )

    def fetch(j, slot, t):
        for which in range(n_pieces):
            pl.when(plan_ref[at + t] == which)(weight_copy(j, t, which, slot).start)

    def hidden_copy(t, ref):
        return pltpu.make_async_copy(
            ref.at[:, pl.ds(pl.multiple_of(plan_ref[at + 2 * count + t], 128), depth)],
            held.at[:, pl.ds(t * depth, depth)],
            held_sem.at[t],
        )

    @pl.when(step == 0)
    def _():
        for t in range(count):
            for code, ref in sources:
                pl.when(plan_ref[at + count + t] == code)(hidden_copy(t, ref).start)
            fetch(0, 0, t)

    slot = lax.rem(step, 2)

    @pl.when(step + 1 < pl.num_programs(0))
    def _():
        for t in range(count):
            fetch(step + 1, 1 - slot, t)

    value = None
    for t in range(count):
        block = pl.ds(t * depth, depth)

        @pl.when(step == 0)
        def _():
            hidden_copy(t, sources[0][1]).wait()

        weight_copy(step, t, 0, slot).wait()
        term = jnp.dot(held[:, block], weights[slot, block], preferred_element_type=jnp.float32)
        value = term if value is None else value + term
    if not final:
        out_ref[...] = value
        return
    mask = mask_ref[...]
    mask = jnp.concatenate([mask] * (tile // mask.shape[1]), axis=1)
    x = jnp.maximum(value + start_ref[...], 0.0) * mask
    totals = []
    for lower, upper in ((0, pass_rows), (pass_rows, x.shape[0])):
        total, slope = pooled(x[lower:upper], groups)
        slope_ref[lower:upper, :] = slope.astype(slope_ref.dtype)
        totals.append(total)
    total = jnp.concatenate(totals, axis=0)
    total_ref[...] = total
    sparse_ref[...] = (jnp.sqrt(jnp.sqrt(total + 1.0)) - 1.0).astype(sparse_ref.dtype)


def forward(found, pieces, plan, at, count, tile=512, pool=None):
    rows = found[0].shape[0]
    depth, width = pieces[0].shape
    keys = sorted(found)
    anywhere = pl.BlockSpec(memory_space=pl.ANY)
    operands = [found[key] for key in keys] + list(pieces)
    in_specs = [anywhere] * len(operands)
    groups = pass_rows = 0
    filled = ()
    if pool is not None:
        start, mask, groups, pass_rows, whole, first, filled = pool
        skip = first // tile
        column = lambda height: pl.BlockSpec((height, tile), lambda j, *_: (0, j + skip))
        operands += [start, mask]
        in_specs.append(pl.BlockSpec((rows, tile), lambda j, *_: (0, j)))
        in_specs.append(pl.BlockSpec(mask.shape, lambda j, *_: (0, 0)))
        in_specs += [anywhere] * len(filled)
        out_shape = [
            jax.ShapeDtypeStruct((rows, whole), jnp.bfloat16),
            jax.ShapeDtypeStruct((2 * groups, whole), jnp.float32),
            jax.ShapeDtypeStruct((2 * groups, width), jnp.bfloat16),
        ]
        part = pl.BlockSpec((2 * groups, tile), lambda j, *_: (0, j))
        out_specs = [column(rows), column(2 * groups), part]
    else:
        out_shape = jax.ShapeDtypeStruct((rows, width), jnp.float32)
        out_specs = pl.BlockSpec((rows, tile), lambda j, *_: (0, j))
    spec = (at, count, tuple(keys), len(pieces), depth, tile, pool is not None, groups, pass_rows, len(filled))
    return pl.pallas_call(
        functools.partial(forward_kernel, spec),
        out_shape=out_shape,
        grid_spec=pltpu.PrefetchScalarGridSpec(
            num_scalar_prefetch=1,
            grid=(width // tile,),
            in_specs=in_specs,
            out_specs=out_specs,
            scratch_shapes=[
                pltpu.VMEM((rows, count * depth), jnp.bfloat16),
                pltpu.VMEM((2, count * depth, tile), jnp.bfloat16),
                pltpu.SemaphoreType.DMA((count,)),
                pltpu.SemaphoreType.DMA((2, count)),
            ],
        ),
        input_output_aliases={1 + len(operands) + i: i for i in range(len(filled))},
        compiler_params=pltpu.CompilerParams(
            dimension_semantics=("arbitrary",), vmem_limit_bytes=VMEM_BYTES
        ),
        cost_estimate=pl.CostEstimate(
            flops=2 * rows * depth * count * width,
            bytes_accessed=count * depth * width * 2 + rows * width * 8,
            transcendentals=rows * width if pool is not None else 0,
        ),
        name="forward_part" if pool is None else "forward_final",
    )(plan, *operands, *filled)


def spans(parts):
    found, lower = [], 0
    for part in parts:
        found.append((lower, part[0].shape[1]))
        lower += part[0].shape[1]
    return found


def first_kernel(spec, plan_ref, slope_ref, pass_ref, query_ref, *refs):
    at, count, ranges, groups, pass_length, query_length, keep = spec
    parts = [refs[i * count : (i + 1) * count] for i in range(len(ranges))]
    refs = refs[count * len(ranges) :]
    (grad_ref, out_ref) = refs[:2] if keep else (refs[1], refs[0])
    held, total, sem = refs[2:]
    step = pl.program_id(0)
    tile = slope_ref.shape[1]
    steps = held.shape[0]

    def copy(j, which):
        i = [i for i, (lower, width) in enumerate(ranges) if lower <= j * tile < lower + width][0]
        return pltpu.make_async_copy(
            parts[i][which].at[:, pl.ds(j * tile - ranges[i][0], tile)], held.at[j], sem.at[j]
        )

    @pl.when(step == 0)
    def _():
        for which in range(count):

            @pl.when(plan_ref[at] == which)
            def _():
                for j in range(steps):
                    copy(j, which).start()

        total[...] = jnp.zeros_like(total)

    lower = 0
    for factor_ref, length in ((pass_ref, pass_length), (query_ref, query_length)):
        for p in range(groups):
            rows = pl.ds(lower, length)
            grad_ref[rows, :] = (slope_ref[rows, :].astype(jnp.float32) * factor_ref[p : p + 1, :]).astype(grad_ref.dtype)
            lower += length
    pltpu.make_async_copy(parts[0][0].at[:, pl.ds(0, tile)], held.at[step], sem.at[step]).wait()
    total[...] += lax.dot_general(
        grad_ref[...], held[step], (((1,), (1,)), ((), ())), preferred_element_type=jnp.float32
    )

    @pl.when(step == steps - 1)
    def _():
        out_ref[...] = total[...].astype(out_ref.dtype)


def backward_first(slopes, factor_pass, factor_query, lengths, parts, plan, at, keep, tile=1024):
    rows, width = slopes.shape
    groups = factor_pass.shape[0]
    depth = parts[0][0].shape[0]
    count = len(parts[0])
    pieces = [piece for part in parts for piece in part]
    column = lambda height: pl.BlockSpec((height, tile), lambda j, *_: (0, j))
    out_shape = [jax.ShapeDtypeStruct((rows, depth), jnp.bfloat16)]
    out_specs = [pl.BlockSpec((rows, depth), lambda j, *_: (0, 0))]
    scratch = [] if keep else [pltpu.VMEM((rows, tile), jnp.bfloat16)]
    if keep:
        out_shape.insert(0, jax.ShapeDtypeStruct((rows, width), jnp.bfloat16))
        out_specs.insert(0, column(rows))
    return pl.pallas_call(
        functools.partial(first_kernel, (at, count, spans(parts), groups) + lengths + (keep,)),
        out_shape=out_shape,
        grid_spec=pltpu.PrefetchScalarGridSpec(
            num_scalar_prefetch=1,
            grid=(width // tile,),
            in_specs=[column(rows), column(groups), column(groups)]
            + [pl.BlockSpec(memory_space=pl.ANY)] * len(pieces),
            out_specs=out_specs,
            scratch_shapes=scratch
            + [
                pltpu.VMEM((width // tile, depth, tile), jnp.bfloat16),
                pltpu.VMEM((rows, depth), jnp.float32),
                pltpu.SemaphoreType.DMA((width // tile,)),
            ],
        ),
        compiler_params=pltpu.CompilerParams(
            dimension_semantics=("arbitrary",), vmem_limit_bytes=FIRST_VMEM_BYTES
        ),
        cost_estimate=pl.CostEstimate(
            flops=2 * rows * depth * width,
            bytes_accessed=(depth * width + 2 * rows * width + rows * depth) * 2,
            transcendentals=0,
        ),
        name="backward_first",
    )(plan, slopes, factor_pass, factor_query, *pieces)


def backward_kernel(spec, plan_ref, slopes_ref, *refs):
    at_plan, count, ranges, parts, adds = spec
    units = len(adds)
    n_adds = max([0] + [i + 1 for unit in adds for i in unit])
    groups = [refs[i * count : (i + 1) * count] for i in range(len(ranges))]
    refs = refs[count * len(ranges) :]
    running, refs = refs[:n_adds], refs[n_adds:]
    outs, (held, slopes, piece_sem, slope_sem) = refs[:units], refs[units:]
    rows = slopes_ref.shape[0] // parts

    def slope_copy(i):
        at = pl.ds(pl.multiple_of(i * rows, 16), rows)
        return pltpu.make_async_copy(slopes_ref.at[at, :], slopes.at[at, :], slope_sem.at[i])

    def piece_copy(unit, i, which):
        lower, width = ranges[i]
        return pltpu.make_async_copy(
            groups[i][which], held.at[unit, :, pl.ds(lower, width)], piece_sem.at[unit, i]
        )

    for unit in range(units):
        for i in range(len(ranges)):
            for which in range(count):
                pl.when(plan_ref[at_plan + unit] == which)(piece_copy(unit, i, which).start)
        if unit == 0:
            for i in range(parts):
                slope_copy(i).start()
    for unit in range(units):
        for i in range(len(ranges)):
            piece_copy(unit, i, 0).wait()

        @pl.loop(0, parts)
        def _(i):
            if unit == 0:
                slope_copy(i).wait()
            at = pl.ds(pl.multiple_of(i * rows, 16), rows)
            value = lax.dot_general(
                slopes[at, :], held[unit], (((1,), (1,)), ((), ())), preferred_element_type=jnp.float32
            ).astype(jnp.bfloat16)
            if adds[unit]:
                value = value.astype(jnp.float32)
                for j in adds[unit]:
                    value = value + running[j][at, :].astype(jnp.float32)
            outs[unit][at, :] = value.astype(outs[unit].dtype)


def backward(slopes, groups, plan, at, running=(), adds=((),)):
    rows, width = slopes.shape
    depth = groups[0][0].shape[0]
    pieces = [piece for group in groups for piece in group]
    count, units = len(groups[0]), len(adds)
    parts = 3 if rows % 48 == 0 else 1
    whole = pl.BlockSpec(memory_space=pltpu.VMEM)
    anywhere = pl.BlockSpec(memory_space=pl.ANY)
    return pl.pallas_call(
        functools.partial(backward_kernel, (at, count, spans(groups), parts, adds)),
        out_shape=[jax.ShapeDtypeStruct((rows, depth), jnp.bfloat16)] * units,
        in_specs=[pl.BlockSpec(memory_space=pltpu.SMEM)] + [anywhere] * (1 + len(pieces)) + [whole] * len(running),
        out_specs=[whole] * units,
        scratch_shapes=[
            pltpu.VMEM((units, depth, width), jnp.bfloat16),
            pltpu.VMEM((rows, width), jnp.bfloat16),
            pltpu.SemaphoreType.DMA((units, len(groups))),
            pltpu.SemaphoreType.DMA((parts,)),
        ],
        compiler_params=pltpu.CompilerParams(vmem_limit_bytes=SMALL_VMEM_BYTES),
        cost_estimate=pl.CostEstimate(
            flops=2 * rows * depth * units * width,
            bytes_accessed=(units * depth * width + rows * width + units * rows * depth) * 2,
            transcendentals=0,
        ),
        name="backward_part",
    )(plan, slopes, *pieces, *running)


def line_reduce_scatter(first, product, n, share):
    left, right = [None] * share, [None] * share
    for step in range(1, n):
        for i in range(share):
            name = f"part{step}_{i}"
            if step == 1 and i < 2:
                to_left = to_right = first(name, i)
            elif 2 * step <= n:
                running = () if step == 1 else (left[i], right[i])
                (to_left,) = product(name, running, (tuple(range(len(running))),))
                to_right = to_left
            else:
                to_left, to_right = product(name, (left[i], right[i]), ((0,), (1,)))
            left[i] = lax.ppermute(to_left, "vocab", [(d, d - 1) for d in range(n - step, n)])
            right[i] = lax.ppermute(to_right, "vocab", [(d, d + 1) for d in range(step)])
    terms = []
    for i in range(share):
        early = i + 1 < share
        running = (left[i], right[i]) if early else ()
        own = product(f"own_{i}", running, (tuple(range(len(running))),))[0]
        if not early:
            own = own.astype(jnp.float32) + left[i].astype(jnp.float32) + right[i].astype(jnp.float32)
        terms.append(own.astype(jnp.bfloat16))
    return terms


def shards(n_vocab, n_rows, *arguments):
    return body(n_vocab, n_rows, *arguments)


def body(n_vocab, n_rows, hidden_pass, hidden_query, mask_pass, mask_query, labels, head_weight):
    groups, pass_length, part = hidden_pass.shape
    query_length = hidden_query.shape[1]
    pass_rows = groups * pass_length
    depth, width = head_weight.shape
    share = n_rows // n_vocab
    plans = Plan(n_vocab, n_rows, depth)
    plan = plans.row()
    order = plan[plans.at["order"] : plans.at["order"] + n_rows]
    tokens = jnp.concatenate(
        [hidden_pass.reshape(pass_rows, part), hidden_query.reshape(groups * query_length, part)], axis=0
    )
    mask = jnp.concatenate([mask_pass.reshape(-1), mask_query.reshape(-1)]).astype(jnp.float32)
    mask = jnp.broadcast_to(mask[:, None], (mask.shape[0], 128))
    found = line_gather(tokens, n_vocab)
    halves = 2 if two_paths(n_rows, n_vocab) and width % 2048 == 0 else 1
    part_width = width // halves
    parts = []
    for i in range(halves):
        own = head_weight
        if i > 0:
            own, _ = lax.optimization_barrier((head_weight, tokens))
        own = own[:, i * part_width : (i + 1) * part_width]
        parts.append(row_gather(own, n_rows, n_vocab))
    all_labels = jnp.stack(row_gather(labels, n_rows, n_vocab)).reshape(-1)
    passages = (order[:, None] * groups + jnp.arange(groups, dtype=jnp.int32)[None, :]).reshape(-1)
    onehot = (all_labels[:, None] == passages[None, :]).astype(jnp.float32)

    half = n_rows // 2
    near, soon = found, n_rows
    if two_paths(n_rows, n_vocab):
        near = {code: block for code, block in found.items() if abs(code) < n_vocab - 1}
        soon = n_rows - 2
    logits, filled, gathered = [], (), []
    for i in range(halves):
        logits.append(forward(near, parts[i][:soon], plan, plans.at["soon"], half))
    for i in range(halves):
        pool = (logits[i], mask, groups, pass_rows, width, i * part_width, filled)
        *filled, sparse = forward(found, parts[i], plan, plans.at["last"], half, pool=pool)
        gathered.append(jnp.stack(row_gather(sparse, n_rows, n_vocab, late=True)))
    slopes, totals = filled
    all_pass = [block[:, :groups].reshape(-1, part_width) for block in gathered]
    all_query = [block[:, groups:].reshape(-1, part_width) for block in gathered]
    scaling = SHARPNESS * (width * n_vocab) ** (-0.5)
    scores = sum(
        lax.dot_general(q, p, (((1,), (1,)), ((), ())), preferred_element_type=jnp.float32)
        for q, p in zip(all_query, all_pass)
    )
    if n_vocab & (n_vocab - 1) == 0:
        hop = 1
        while hop < n_vocab:
            scores = scores + lax.ppermute(scores, "vocab", [(d, d ^ hop) for d in range(n_vocab)])
            hop *= 2
    else:
        scores = lax.psum(scores, "vocab")
    scores = scores * scaling
    positive = jnp.sum(scores * onehot, axis=1, keepdims=True)
    weights = jax.nn.sigmoid(MARGIN + scores - positive) * (1.0 - onehot)
    score_grad = ((weights - onehot * jnp.sum(weights, axis=1, keepdims=True)) * scaling).astype(jnp.bfloat16)
    if two_paths(n_rows, n_vocab):
        of_query, of_pass = score_grad[:groups], score_grad[:, :groups]
    else:
        row = lax.axis_index("rows") * groups
        of_query = lax.dynamic_slice_in_dim(score_grad, row, groups, 0)
        of_pass = lax.dynamic_slice_in_dim(score_grad, row, groups, 1)
    query_grad = jnp.concatenate(
        [jnp.dot(of_query, p, preferred_element_type=jnp.float32) for p in all_pass], axis=1
    )
    pass_grad = jnp.concatenate(
        [
            lax.dot_general(of_pass, q, (((0,), (0,)), ((), ())), preferred_element_type=jnp.float32)
            for q in all_query
        ],
        axis=1,
    )
    root = jnp.sqrt(jnp.sqrt(totals + 1.0))
    cube = root * root * root
    factors = (pass_grad / cube[:groups], query_grad / cube[groups:], (pass_length, query_length))
    logit_grad = []

    def first(name, i):
        keep = i == 1 or share == 1
        *grad, block = backward_first(slopes, *factors, parts, plan, plans.at[name], keep)
        logit_grad.extend(grad)
        return block

    def product(name, running, adds):
        return backward(logit_grad[0], parts, plan, plans.at[name], running, adds)

    summed = line_reduce_scatter(first, product, n_vocab, share)
    summed = jnp.concatenate(summed, axis=1)
    return (
        summed[:pass_rows].reshape(groups, pass_length, part),
        summed[pass_rows:].reshape(groups, query_length, part),
    )


def solution(mesh):
    n_vocab, n_rows = mesh.shape["vocab"], mesh.shape["rows"]
    return jax.shard_map(
        functools.partial(shards, n_vocab, n_rows),
        mesh=mesh,
        in_specs=(
            P("rows", None, "vocab"),
            P("rows", None, "vocab"),
            P("rows", None),
            P("rows", None),
            P("rows"),
            P("rows", "vocab"),
        ),
        out_specs=(P("rows", None, "vocab"), P("rows", None, "vocab")),
        check_vma=False,
    )
```
